256 devices in a mesh: sess: 32 (over x_hi, z, core), exp: 8 (over y, x_lo).
Axes of the slice: x: 4 (x_hi: 2, x_lo: 2; x = x_hi * 2 + x_lo), y: 4, z: 8, core: 2. Of those that a mesh axis runs over, the one named last changes fastest.
Arguments:
- tokens: bfloat16 [32, 256, 4096], P('sess'), may hold values from -6 to 6
- routes: int32 [32, 256, 2], P('sess'), may hold values from 0 to 31, all different within a row; in each aligned block of 256 rows (0 to 255, 256 to 511, ..., all dimensions but the last counted through in order) at most 32 rows name the same one
- gates: float32 [32, 256, 2], P('sess'), may hold values from 0.2 to 1
- w_gate: bfloat16 [32, 4096, 1408], P('sess', None, 'exp'), may hold values from -0.09375 to 0.09375
- w_up: bfloat16 [32, 4096, 1408], P('sess', None, 'exp'), may hold values from -0.09375 to 0.09375
- w_down: bfloat16 [32, 1408, 4096], P('sess', 'exp'), may hold values from -0.15625 to 0.15625
- feat_gain: float32 [4096], replicated, may hold values from 0.25 to 1.75
- w_proj: bfloat16 [4096, 256], replicated, may hold values from -0.09375 to 0.09375
- conv_time: bfloat16 [3, 3, 3, 256, 256], replicated, may hold values from -0.078125 to 0.078125
- bias_time: float32 [256], replicated, may hold values from -3 to 3
- conv_space: bfloat16 [3, 3, 256, 256], replicated, may hold values from -0.125 to 0.125
- bias_space: float32 [256], replicated, may hold values from -3 to 3
- frame_cache: bfloat16 [3, 32, 64, 16, 256], P(None, 'sess', 'exp'), may hold values from -6 to 6
- cache_head: int32 [32], P('sess'), may hold values from 0 to 2
Outputs:
- out_frame: bfloat16 [32, 64, 16, 256], P('sess', 'exp')
The draws below stay inside these ranges and needn't reach their ends.
Inputs may be any that keep to these rules, and one draw needn't show every extreme that they name: `routes`: each token names 2 different experts; among the tokens of one session no expert is named more than 32 times, and in some sessions one is named exactly 32 times. The frame before the previous one is in slot (cache_head + 2) mod 3.
All inputs are finite; a program needn't handle non-finite values.
Results may differ from the reference program's by a relative error of at most 0.017.
Values may be sent and summed in bfloat16 or wider, within the bound.
No kernel may reach another device: no remote copies, remote signals or barrier semaphores. Data moves between devices by JAX's collectives and lax.ppermute only.
A program may use at most 64 MiB of HBM per device.

```python
import math
import jax
import jax.numpy as jnp
import numpy as np
from jax import lax

D = 4096
HID = 1408
C = 256
TOPK = 2
GRID_W = 8
EXPERTS = 32
SESS = 32
GRID_H = 32
TOK_SESS = 256
CAP = 32
PH = 64
PW = 16
N_EXP = 8


def set_ends(drawn, key, low, largest):
    extent = drawn.shape
    place = [jax.random.randint(jax.random.fold_in(key, axis), (), 0, extent[axis]) for axis in range(len(extent))]
    drawn = drawn.at[tuple(place)].set(low)
    longest = extent.index(max(extent))
    place[longest] = (place[longest] + 1) % extent[longest]
    return drawn.at[tuple(place)].set(largest)


def block_levels(rng, extent, cuts, smallest, top_value):
    gain, own = 1.0, jax.random.fold_in(rng, 6)
    for dim, shards_of in cuts:
        draws = jnp.exp(jax.random.uniform(jax.random.fold_in(own, dim), (shards_of,), jnp.float32, smallest / len(cuts), top_value / len(cuts)))
        gain = gain * jnp.repeat(draws, extent[dim] // shards_of).reshape([-1 if axis == dim else 1 for axis in range(len(extent))])
    return gain


def shared_out(rng, own, number, rows, number_of, top, reach, slope):
    ranking = jax.random.permutation(rng, number_of)
    crowded, usual = portions_of(number_of, rows * top, reach, slope, True), portions_of(number_of, rows * top, reach, slope, False)
    places = jnp.arange(number_of)

    def named(lengths, turn):
        used = int((lengths > 0).sum())
        fixed = max(1, used // 4)
        shifted = fixed + (places - fixed + turn * (used - fixed)) % max(1, number_of - fixed)
        return jnp.zeros((number_of,), jnp.int32).at[ranking[jnp.where(places < fixed, places, shifted)]].set(jnp.asarray(lengths, jnp.int32))

    lengths = jnp.where(number % 4 == 0, named(crowded, number // 4), named(usual, number - number // 4 - 1))
    mixed = jax.random.permutation(jax.random.fold_in(own, 3), number_of)
    giver, sink = mixed[0:number_of // 2 * 2:2], mixed[1:number_of // 2 * 2:2]
    slack = jnp.minimum(lengths[giver] - 1, reach - lengths[sink]) // 2
    slack = jnp.where((giver == ranking[0]) | (sink == ranking[0]) | (lengths[sink] == 0), 0, jnp.maximum(slack, 0))
    shifted = jax.random.randint(jax.random.fold_in(own, 4), (number_of // 2,), 0, 1 << 20) % (slack + 1)
    lengths = lengths.at[giver].add(-shifted).at[sink].add(shifted)
    members = jnp.searchsorted(jnp.cumsum(lengths), jnp.arange(rows * top), side="right").astype(jnp.int32)
    table = members.reshape(top, rows).T
    table = table[jax.random.permutation(jax.random.fold_in(own, 1), rows)]
    turn = jax.random.randint(jax.random.fold_in(own, 2), (rows, 1), 0, top)
    return jnp.take_along_axis(table, (jnp.arange(top)[None, :] + turn) % top, axis=1)


def portions_of(number_of, total, limit, lean, full):
    weights = [(1 << 20) // math.isqrt(rank ** lean) + 1 for rank in range(1, number_of + 1)]
    largest = limit if full else min(limit, max(-(-total // number_of), total * weights[0] // sum(weights)))
    least = 1 if total - largest >= number_of - 1 else 0
    counts, spare = [largest] + [least] * (number_of - 1), total - largest - least * (number_of - 1)
    while spare > 0:
        movable = [i for i in range(1, number_of) if counts[i] < largest] or [i for i in range(1, number_of) if counts[i] < limit]
        whole, budget = sum([weights[i] for i in movable]), spare
        for i in movable:
            addition = min(limit - counts[i], max(1, budget * weights[i] // whole), spare)
            counts[i] = counts[i] + addition
            spare = spare - addition
    return np.array(counts)


def centred(rng, extent, scale, limit, cuts=(), kind=jnp.bfloat16):
    values = jax.random.normal(rng, extent, jnp.float32) * scale
    if len(cuts) > 0:
        values = block_levels(rng, extent, cuts, -0.22, 0.18) * values
    return jnp.clip(values, min=-limit, max=limit).astype(kind)


def setup_inputs(seed: int = 0) -> dict:
    keys = jax.random.split(jax.random.key(seed), 15)
    tokens = centred(keys[0], (SESS, TOK_SESS, D), 1.0, 6.0, ((0, 32),))
    routes_keys = jax.random.split(jax.random.fold_in(keys[1], 1), SESS * TOK_SESS // TOK_SESS)
    routes_turns = jax.random.permutation(jax.random.fold_in(keys[1], 3), SESS * TOK_SESS // TOK_SESS)
    routes = jax.vmap(lambda own, number: shared_out(jax.random.fold_in(keys[1], 2), own, number, TOK_SESS, EXPERTS, TOPK, CAP, 2))(routes_keys, routes_turns).reshape((SESS, TOK_SESS, TOPK))
    gates = jnp.clip(0.2 + 0.8 * jax.random.uniform(keys[2], (SESS, TOK_SESS, TOPK), jnp.float32) ** block_levels(keys[2], (SESS, TOK_SESS, TOPK), ((0, 32),), -0.2, 0.2), 0.2, 1.0)
    w_gate = centred(keys[3], (EXPERTS, D, HID), D ** -0.5, 0.09375, ((0, 32), (2, 8)))
    w_up = centred(keys[4], (EXPERTS, D, HID), D ** -0.5, 0.09375, ((0, 32), (2, 8)))
    w_down = centred(keys[5], (EXPERTS, HID, D), HID ** -0.5, 0.15625, ((0, 32), (1, 8)))
    feat_gain = jnp.clip(1.0 + 0.15 * jax.random.normal(keys[6], (D,), jnp.float32), 0.25, 1.75)
    w_proj = centred(keys[7], (D, C), D ** -0.5, 0.09375)
    conv_time = centred(keys[8], (3, 3, 3, C, C), (27 * C) ** -0.5, 0.078125)
    bias_time = centred(keys[9], (C,), 0.5, 3.0, (), jnp.float32)
    conv_space = centred(keys[10], (3, 3, C, C), (9 * C) ** -0.5, 0.125)
    bias_space = centred(keys[11], (C,), 0.5, 3.0, (), jnp.float32)
    frame_cache = centred(keys[12], (3, SESS, PH, PW, C), 1.0, 6.0, ((1, 32), (2, 8)))
    cache_head = set_ends(jax.random.randint(keys[13], (SESS,), 0, 3), jax.random.fold_in(keys[13], 1), 0, 2).astype(jnp.int32)
    return {"tokens": tokens, "routes": routes, "gates": gates, "w_gate": w_gate, "w_up": w_up, "w_down": w_down, "feat_gain": feat_gain, "w_proj": w_proj, "conv_time": conv_time, "bias_time": bias_time, "conv_space": conv_space, "bias_space": bias_space, "frame_cache": frame_cache, "cache_head": cache_head}


epsilon = 1e-06

def slot_targets(routes, experts, capacity):
    flat = routes.reshape(-1).astype(jnp.int32)
    onehot = (flat[:, None] == jnp.arange(experts, dtype=jnp.int32)[None, :]).astype(jnp.int32)
    before = jnp.cumsum(onehot, axis=0) - onehot
    position = lax.optimization_barrier(jnp.sum(before * onehot, axis=1))
    return (flat * capacity + position).astype(jnp.int32)

def pick_slot(cache, heads):
    choose = (jnp.arange(3, dtype=jnp.int32)[:, None] == heads[None, :]).astype(jnp.float32)
    return lax.optimization_barrier(jnp.sum(choose[:, :, None, None, None] * cache.astype(jnp.float32), axis=0)).astype(jnp.bfloat16)

def reference(tokens, routes, gates, w_gate, w_up, w_down, feat_gain, w_proj, conv_time, bias_time, conv_space, bias_space, frame_cache, cache_head):
    capacity = CAP
    slots = EXPERTS * capacity
    count = TOK_SESS * TOPK
    slice_width = HID // N_EXP
    dest = jax.vmap(lambda single: slot_targets(single, EXPERTS, capacity))(routes)
    filler = jnp.full((SESS, slots), count, jnp.int32)
    owner = jax.vmap(lambda base, target: base.at[target].set(jnp.arange(count, dtype=jnp.int32)))(filler, dest)
    padded = jnp.concatenate([tokens, jnp.zeros((SESS, 1, D), tokens.dtype)], axis=1)
    weights = jnp.concatenate([gates.reshape(SESS, count), jnp.zeros((SESS, 1), jnp.float32)], axis=1)
    session_ids = jnp.arange(SESS, dtype=jnp.int32)[:, None]

    def one_expert(total, expert):
        route_ids = lax.dynamic_slice_in_dim(owner, (expert * capacity).astype(jnp.int32), capacity, 1)
        token_ids = jnp.where(route_ids < count, route_ids // TOPK, TOK_SESS).astype(jnp.int32)
        rows = padded[session_ids, token_ids].reshape(SESS * capacity, D)
        gate = jnp.dot(rows, w_gate[expert], preferred_element_type=jnp.float32)
        upward = jnp.dot(rows, w_up[expert], preferred_element_type=jnp.float32)
        hidden = (jax.nn.silu(gate) * upward).astype(jnp.bfloat16)
        pieces = hidden.astype(jnp.float32).reshape(-1, N_EXP, slice_width)
        lowered = w_down[expert].astype(jnp.float32).reshape(N_EXP, slice_width, D)
        parts = jnp.einsum('rjh,jhd->rjd', pieces, lowered).astype(jnp.bfloat16)
        summed = lax.optimization_barrier(jnp.sum(parts.astype(jnp.float32), axis=1)).reshape(SESS, capacity, D)
        scale = weights[session_ids, route_ids]
        total = total.at[session_ids, token_ids].add(scale[:, :, None] * summed)
        return (total, None)
    start_total = jnp.zeros((SESS, TOK_SESS + 1, D), jnp.float32)
    total, _ = lax.scan(one_expert, start_total, jnp.arange(EXPERTS, dtype=jnp.int32))
    mixed = total[:, :TOK_SESS]
    feat = (tokens.astype(jnp.float32) + mixed).astype(jnp.bfloat16)
    square = lax.optimization_barrier(jnp.mean(jnp.square(feat.astype(jnp.float32)), axis=-1, keepdims=True))
    normed = (feat.astype(jnp.float32) * lax.rsqrt(square + epsilon) * feat_gain).astype(jnp.bfloat16)
    coarse = jnp.dot(normed.reshape(-1, D), w_proj, preferred_element_type=jnp.float32).astype(jnp.bfloat16)
    coarse = coarse.reshape(SESS, GRID_H, GRID_W, C)
    fine = jnp.repeat(jnp.repeat(coarse, 2, axis=1), 2, axis=2)
    latest = pick_slot(frame_cache, cache_head)
    older = pick_slot(frame_cache, (cache_head + 2) % 3)
    stack = jnp.stack([older, latest, fine])
    framed = jnp.pad(stack, ((0, 0), (0, 0), (1, 1), (1, 1), (0, 0)))
    first = jnp.zeros((SESS * PH * PW, C), jnp.float32)
    for frame_step in range(3):
        for row_step in range(3):
            for col_step in range(3):
                patch = framed[frame_step, :, row_step:row_step + PH, col_step:col_step + PW, :].reshape(-1, C)
                first = first + jnp.dot(patch, conv_time[frame_step, row_step, col_step], preferred_element_type=jnp.float32)
    active = jax.nn.silu(first + bias_time).astype(jnp.bfloat16).reshape(SESS, PH, PW, C)
    bordered = jnp.pad(active, ((0, 0), (1, 1), (1, 1), (0, 0)))
    second = jnp.zeros((SESS * PH * PW, C), jnp.float32)
    for row_step in range(3):
        for col_step in range(3):
            patch = bordered[:, row_step:row_step + PH, col_step:col_step + PW, :].reshape(-1, C)
            second = second + jnp.dot(patch, conv_space[row_step, col_step], preferred_element_type=jnp.float32)
    result = fine.astype(jnp.float32).reshape(-1, C) + second + bias_space
    return result.astype(jnp.bfloat16).reshape(SESS, PH, PW, C)
```

```python
import jax
import jax.numpy as jnp
from jax import lax
from jax.experimental import pallas as pl
from jax.experimental.pallas import tpu as pltpu
from jax.sharding import Mesh
from jax.sharding import PartitionSpec as P

EXP = ("yh", "yl", "x")
EPS = 1e-06
F32 = jnp.float32
BF16 = jnp.bfloat16
PARAMS = pltpu.CompilerParams(vmem_limit_bytes=48 * 1024 * 1024)


def whole(shape):
    zeros = (0,) * len(shape)
    return pl.BlockSpec(shape, lambda i, s: zeros)


def call(kernel, name, scalars, operands, specs, outs, scratch=(), aliases=None):
    single = not isinstance(outs, (list, tuple))
    out_list = [outs] if single else list(outs)
    result = pl.pallas_call(
        kernel,
        name=name,
        out_shape=out_list,
        grid_spec=pltpu.PrefetchScalarGridSpec(
            num_scalar_prefetch=1,
            grid=(1,),
            in_specs=specs,
            out_specs=[whole(o.shape) for o in out_list],
            scratch_shapes=list(scratch),
        ),
        compiler_params=PARAMS,
        input_output_aliases=aliases or {},
    )(scalars, *operands)
    return result[0] if single else result


def iota(shape, dim):
    return lax.broadcasted_iota(jnp.int32, shape, dim)


def dispatch_kernel(sc, routes_ref, gates_ref, tok_ref, out_ref, col_ref):
    half = sc[1]
    count = routes_ref.shape[1]
    rows = out_ref.shape[0]
    experts = iota((32, count), 0)
    first = routes_ref[0:1, :]
    second = routes_ref[1:2, :]
    is_first = experts == first
    is_second = experts == second
    named = jnp.where(is_first | is_second, 1.0, 0.0).astype(BF16)
    earlier = jnp.where(iota((count, count), 0) < iota((count, count), 1), 1.0, 0.0).astype(BF16)
    before = jnp.dot(named, earlier, preferred_element_type=F32)
    pos_a = jnp.sum(jnp.where(is_first, before, 0.0), axis=0, keepdims=True).astype(jnp.int32)
    pos_b = jnp.sum(jnp.where(is_second, before, 0.0), axis=0, keepdims=True).astype(jnp.int32)
    place_a = (pos_a >> 4) * rows + first * 16 + (pos_a & 15)
    place_b = (pos_b >> 4) * rows + second * 16 + (pos_b & 15)
    slot = iota((rows, count), 0) + half * rows
    pick = jnp.where((slot == place_a) | (slot == place_b), 1.0, 0.0).astype(BF16)
    out_ref[...] = jnp.dot(pick, tok_ref[...], preferred_element_type=F32).astype(BF16)
    line = iota((128, count), 0)
    table = jnp.where(
        line == 0,
        place_a.astype(F32),
        jnp.where(
            line == 1,
            place_b.astype(F32),
            jnp.where(line == 2, gates_ref[0:1, :], jnp.where(line == 3, gates_ref[1:2, :], 0.0)),
        ),
    )
    col_ref[...] = table.T


def weights_kernel(sc, col_ref, high_ref, low_ref):
    slot = iota(high_ref.shape, 1)
    place_a = col_ref[:, 0:1].astype(jnp.int32)
    place_b = col_ref[:, 1:2].astype(jnp.int32)
    gate = jnp.where(slot == place_a, col_ref[:, 2:3], 0.0) + jnp.where(
        slot == place_b, col_ref[:, 3:4], 0.0
    )
    high = gate.astype(BF16)
    high_ref[...] = high
    low_ref[...] = (gate - high.astype(F32)).astype(BF16)


def product(rows, weights):
    return lax.dot_general(rows, weights, (((1,), (1,)), ((), ())), preferred_element_type=F32)


def joined_weights(refs, gate_w, up_w):
    own_gate, other_gate, own_up, other_up = refs
    part = own_gate.shape[0]
    gate_w[0:part, :] = own_gate[...]
    gate_w[part : 2 * part, :] = other_gate[...]
    up_w[0:part, :] = own_up[...]
    up_w[part : 2 * part, :] = other_up[...]


def start_kernel(sc, x_ref, w0, w1, w2, w3, gate_ref, up_ref, gate_w, up_w):
    joined_weights((w0, w1, w2, w3), gate_w, up_w)
    gate_ref[...] = product(x_ref[...], gate_w[...])
    up_ref[...] = product(x_ref[...], up_w[...])


def more_kernel(sc, x_ref, w0, w1, w2, w3, gate_in, up_in, gate_ref, up_ref, gate_w, up_w):
    joined_weights((w0, w1, w2, w3), gate_w, up_w)
    gate_ref[...] = gate_in[...] + product(x_ref[...], gate_w[...])
    up_ref[...] = up_in[...] + product(x_ref[...], up_w[...])


def last_kernel(sc, top_ref, low_ref, w0, w1, w2, w3, gate_in, up_in, out_ref, gate_w, up_w):
    joined_weights((w0, w1, w2, w3), gate_w, up_w)
    middle = top_ref.shape[0]
    for ref, begin in ((top_ref, 0), (low_ref, middle)):
        rows = slice(begin, begin + middle)
        gate = gate_in[rows, :] + product(ref[...], gate_w[...])
        up = up_in[rows, :] + product(ref[...], up_w[...])
        out_ref[rows, :] = (gate / (1.0 + jnp.exp(-gate)) * up).astype(BF16)


def down_kernel(sc, h0, h1, h2, h3, wd_ref, out_ref):
    share = out_ref.shape[2]
    for part in range(2):
        cols = slice(part * share, (part + 1) * share)
        total = jnp.dot(h0[...], wd_ref[0, :, cols], preferred_element_type=F32)
        total += jnp.dot(h1[...], wd_ref[1, :, cols], preferred_element_type=F32)
        total += jnp.dot(h2[...], wd_ref[2, :, cols], preferred_element_type=F32)
        total += jnp.dot(h3[...], wd_ref[3, :, cols], preferred_element_type=F32)
        out_ref[part] = total.astype(BF16)


def combine_kernel(sc, ret_ref, high_ref, low_ref, tok_ref, gain_ref, proj_ref, out_ref):
    mixed = jnp.dot(high_ref[...], ret_ref[...], preferred_element_type=F32)
    mixed += jnp.dot(low_ref[...], ret_ref[...], preferred_element_type=F32)
    feat = (tok_ref[...].astype(F32) + mixed).astype(BF16).astype(F32)
    square = jnp.sum(feat * feat, axis=1, keepdims=True)
    part = jnp.dot(
        (feat * gain_ref[...]).astype(BF16), proj_ref[...], preferred_element_type=F32
    )
    tiles, block, _ = out_ref.shape
    count, channels = part.shape
    lane = iota((count, 128), 1)
    high = square.astype(BF16).astype(F32)
    extra = jnp.where(lane == 0, high, jnp.where(lane == 1, square - high, 0.0))
    own = count // tiles
    border = (block - own) // 2
    for tile in range(tiles):
        begin = tile * own - border
        low, top = max(begin, 0), min(begin + block, count)
        for value, cols in (
            (part, slice(0, channels)),
            (extra, slice(channels, channels + 128)),
        ):
            pieces = [value[low:top, :]]
            if low > begin:
                pieces = [jnp.zeros((low - begin, value.shape[1]), F32)] + pieces
            if top < begin + block:
                pieces = pieces + [jnp.zeros((begin + block - top, value.shape[1]), F32)]
            joined = pieces[0] if len(pieces) == 1 else jnp.concatenate(pieces, axis=0)
            out_ref[tile, :, cols] = joined.astype(BF16)


def convolved(field, weights, rows):
    sums = []
    for col_step in range(3):
        total = None
        for row_step in range(3):
            term = jnp.dot(
                field[row_step * 16 : row_step * 16 + rows, :],
                weights(row_step, col_step),
                preferred_element_type=F32,
            )
            total = term if total is None else total + term
        sums.append(total)
    col = iota(sums[0].shape, 0) & 15
    left = jnp.where(col == 0, 0.0, pltpu.roll(sums[0], 1, 0))
    right = jnp.where(col == 15, 0.0, pltpu.roll(sums[2], rows - 1, 0))
    return sums[1] + left + right


def cache_kernel(sc, cache_ref, above_ref, below_ref, weight_ref, bias_ref, out_ref):
    head = sc[2]
    older = lax.rem(head + 2, 3)
    total = jnp.broadcast_to(bias_ref[...], out_ref.shape)
    for step, slot in ((0, older), (1, head)):
        field = jnp.concatenate([above_ref[slot], cache_ref[slot], below_ref[slot]], axis=0)
        total = total + convolved(field, lambda r, c: weight_ref[step, r, c], out_ref.shape[0])
    out_ref[...] = total


def tail_kernel(sc, arr_ref, past_ref, time_ref, space_ref, bias_ref, out_ref):
    tile = sc[0]
    total = arr_ref[0].astype(F32)
    for source in range(1, arr_ref.shape[0]):
        total = total + arr_ref[source].astype(F32)
    channels = out_ref.shape[1]
    square = total[:, channels : channels + 1] + total[:, channels + 1 : channels + 2]
    scale = lax.rsqrt(square / 4096.0 + EPS)
    coarse = (total[:, :channels] * scale).astype(BF16)
    block = coarse.shape[0]
    pixel = iota((4 * block, block), 0)
    spread = jnp.where(
        iota((4 * block, block), 1) == (pixel >> 5) * 8 + ((pixel & 15) >> 1), 1.0, 0.0
    ).astype(BF16)
    fine = jnp.dot(spread, coarse, preferred_element_type=F32)
    field = fine.astype(BF16)
    rows = past_ref.shape[0]
    first = past_ref[...] + convolved(field, lambda r, c: time_ref[0, r, c], rows)
    active = first / (1.0 + jnp.exp(-first))
    place = (iota(active.shape, 0) >> 4) + tile * 8 - 1
    active = jnp.where((place >= 0) & (place < 64), active, 0.0).astype(BF16)
    own = out_ref.shape[0]
    second = convolved(active, lambda r, c: space_ref[r, c], own)
    out_ref[...] = (fine[32 : 32 + own, :] + second + bias_ref[...]).astype(BF16)


def swapped(x, axis):
    return lax.ppermute(x, axis, [(0, 1), (1, 0)])


def body(
    tokens,
    routes,
    gates,
    w_gate,
    w_up,
    w_down,
    feat_gain,
    w_proj,
    conv_time,
    bias_time,
    conv_space,
    bias_space,
    frame_cache,
    cache_head,
):
    tile = lax.axis_index(EXP).astype(jnp.int32)
    half, quarter = tile >> 2, tile & 3
    scalars = jnp.stack([tile, half, cache_head[0], quarter, quarter ^ 1, quarter ^ 2, quarter ^ 3])
    count, width = tokens.shape[1:]
    hid = w_gate.shape[2]
    channels = w_proj.shape[1]
    fourth = width // 4
    share = width // 8
    own_gate, own_up = w_gate[0].T, w_up[0].T

    with jax.named_scope("exchange_weights"):
        pairs = [(i, i ^ 6) for i in range(8)]
        other_gate = lax.ppermute(own_gate, EXP, pairs)
        other_up = lax.ppermute(own_up, EXP, pairs)
        slabs = jnp.moveaxis(w_down[0].reshape(hid, 4, fourth), 1, 0)
        slabs = jnp.concatenate([slabs, slabs], axis=0)
        down = lax.all_to_all(slabs, EXP, 0, 0, tiled=True)
        order = [tile, tile ^ 6, tile ^ 2, tile ^ 4, tile ^ 1, tile ^ 7, tile ^ 3, tile ^ 5]
        down = jnp.concatenate(
            [lax.dynamic_slice_in_dim(down, i, 1, 0) for i in order], axis=0
        ).reshape(4, 2 * hid, fourth)

    with jax.named_scope("cache"):
        frames = frame_cache.reshape(3, 128, channels)
        above = lax.ppermute(frames[:, 96:], EXP, [(i, i + 1) for i in range(7)])
        below = lax.ppermute(frames[:, :32], EXP, [(i + 1, i) for i in range(7)])
        past = call(
            cache_kernel,
            "cache",
            scalars,
            (frames, above, below, conv_time, bias_time.reshape(1, channels)),
            [
                whole(frames.shape),
                whole(above.shape),
                whole(below.shape),
                pl.BlockSpec((2, 3, 3, channels, channels), lambda i, s: (0, 0, 0, 0, 0)),
                whole((1, channels)),
            ],
            jax.ShapeDtypeStruct((160, channels), F32),
        )

    with jax.named_scope("dispatch"):
        outgoing, columns = call(
            dispatch_kernel,
            "dispatch",
            scalars,
            (routes[0].T, gates[0].T, tokens[0]),
            [
                whole((2, count)),
                whole((2, count)),
                pl.BlockSpec((count, fourth), lambda i, s: (0, s[3])),
            ],
            [
                jax.ShapeDtypeStruct((512, fourth), BF16),
                jax.ShapeDtypeStruct((count, 128), F32),
            ],
        )
        arrived = lax.all_to_all(
            outgoing.reshape(32, 16, fourth), "sess", 0, 0, tiled=True
        ).reshape(512, fourth)
        high, low = call(
            weights_kernel,
            "weights",
            scalars,
            (columns,),
            [whole((count, 128))],
            [jax.ShapeDtypeStruct((count, 1024), BF16)] * 2,
        )

    with jax.named_scope("gather"):
        from_y = swapped(arrived, "yl")
        from_x = swapped(arrived, "x")
        corner_top = swapped(from_y[:256], "x")
        corner_low = swapped(from_x[256:], "yl")

    with jax.named_scope("experts"):
        weights = (own_gate, other_gate, own_up, other_up)
        pair = [jax.ShapeDtypeStruct((512, 2 * hid), F32)] * 2
        scratch = [pltpu.VMEM((2 * hid, fourth), BF16)] * 2
        rows = whole((512, fourth))
        acc = whole((512, 2 * hid))

        def columns_of(which):
            return [pl.BlockSpec((hid, fourth), lambda i, s: (0, s[which]))] * 4

        gate, up = call(
            start_kernel, "start", scalars, (arrived, *weights), [rows] + columns_of(3), pair, scratch
        )
        for name, piece, which in (("from_x", from_x, 4), ("from_y", from_y, 5)):
            gate, up = call(
                more_kernel,
                name,
                scalars,
                (piece, *weights, gate, up),
                [rows] + columns_of(which) + [acc, acc],
                pair,
                scratch,
                {6: 0, 7: 1},
            )
        hidden = call(
            last_kernel,
            "hidden",
            scalars,
            (corner_top, corner_low, *weights, gate, up),
            [whole((256, fourth))] * 2 + columns_of(6) + [acc, acc],
            jax.ShapeDtypeStruct((512, 2 * hid), BF16),
            scratch,
        )

    with jax.named_scope("hidden_gather"):
        hidden_y = swapped(hidden, "yl")
        hidden_x = swapped(hidden, "x")
        hidden_c = lax.ppermute(hidden, ("yl", "x"), [(i, 3 - i) for i in range(4)])

    with jax.named_scope("down"):
        answer = call(
            down_kernel,
            "down",
            scalars,
            (hidden, hidden_y, hidden_x, hidden_c, down),
            [whole((512, 2 * hid))] * 4 + [whole(down.shape)],
            jax.ShapeDtypeStruct((2, 512, share), BF16),
        )
        returned = lax.all_to_all(
            answer.reshape(64, 16, share), ("yh", "sess"), 0, 0, tiled=True
        ).reshape(1024, share)

    with jax.named_scope("combine"):
        blocks = call(
            combine_kernel,
            "combine",
            scalars,
            (returned, high, low, tokens[0], feat_gain.reshape(1, width), w_proj),
            [
                whole((1024, share)),
                whole((count, 1024)),
                whole((count, 1024)),
                pl.BlockSpec((count, share), lambda i, s: (0, s[3] * 2 + s[1])),
                pl.BlockSpec((1, share), lambda i, s: (0, s[3] * 2 + s[1])),
                pl.BlockSpec((share, channels), lambda i, s: (s[3] * 2 + s[1], 0)),
            ],
            jax.ShapeDtypeStruct((8, 48, channels + 128), BF16),
        )
        blocks = lax.all_to_all(blocks, EXP, 0, 0, tiled=True)

    with jax.named_scope("decode"):
        out = call(
            tail_kernel,
            "decode",
            scalars,
            (blocks, past, conv_time, conv_space, bias_space.reshape(1, channels)),
            [
                whole(blocks.shape),
                whole((160, channels)),
                pl.BlockSpec((1, 3, 3, channels, channels), lambda i, s: (2, 0, 0, 0, 0)),
                whole(conv_space.shape),
                whole((1, channels)),
            ],
            jax.ShapeDtypeStruct((128, channels), BF16),
        )
    return out.reshape(1, 8, 16, channels)


def solution(mesh):
    finer = Mesh(
        mesh.devices.reshape(mesh.shape["sess"], 2, 2, 2), ("sess", "yh", "yl", "x")
    )
    return jax.shard_map(
        body,
        mesh=finer,
        in_specs=(
            P("sess", None, None),
            P("sess", None, None),
            P("sess", None, None),
            P("sess", None, EXP),
            P("sess", None, EXP),
            P("sess", EXP, None),
            P(),
            P(),
            P(),
            P(),
            P(),
            P(),
            P(None, "sess", EXP, None, None),
            P("sess"),
        ),
        out_specs=P("sess", EXP, None, None),
        check_vma=False,
    )
```

```python
import jax
import jax.numpy as jnp
from jax import lax
from jax.experimental import pallas as pl
from jax.experimental.pallas import tpu as pltpu
from jax.sharding import Mesh
from jax.sharding import PartitionSpec as P

EXP = ("yh", "yl", "x")
EPS = 1e-06
F32 = jnp.float32
BF16 = jnp.bfloat16


def whole(shape):
    zeros = (0,) * len(shape)
    return pl.BlockSpec(shape, lambda i, s: zeros)


def call(kernel, name, scalars, operands, specs, outs, scratch=(), limit=12, cost=None):
    single = not isinstance(outs, (list, tuple))
    out_list = [outs] if single else list(outs)
    result = pl.pallas_call(
        kernel,
        name=name,
        out_shape=out_list,
        grid_spec=pltpu.PrefetchScalarGridSpec(
            num_scalar_prefetch=1,
            grid=(1,),
            in_specs=specs,
            out_specs=[whole(o.shape) for o in out_list],
            scratch_shapes=list(scratch),
        ),
        compiler_params=pltpu.CompilerParams(vmem_limit_bytes=limit * 1024 * 1024),
        cost_estimate=cost,
    )(scalars, *operands)
    return result[0] if single else result


def iota(shape, dim):
    return lax.broadcasted_iota(jnp.int32, shape, dim)


def dispatch_kernel(sc, routes_ref, gates_ref, tok_ref, out_ref, col_ref):
    half = sc[1]
    count = routes_ref.shape[1]
    rows = out_ref.shape[0]
    experts = iota((32, count), 0)
    first = routes_ref[0:1, :]
    second = routes_ref[1:2, :]
    is_first = experts == first
    is_second = experts == second
    named = jnp.where(is_first | is_second, 1.0, 0.0).astype(BF16)
    earlier = jnp.where(iota((count, count), 0) < iota((count, count), 1), 1.0, 0.0).astype(BF16)
    before = jnp.dot(named, earlier, preferred_element_type=F32)
    pos_a = jnp.sum(jnp.where(is_first, before, 0.0), axis=0, keepdims=True).astype(jnp.int32)
    pos_b = jnp.sum(jnp.where(is_second, before, 0.0), axis=0, keepdims=True).astype(jnp.int32)
    place_a = (pos_a >> 4) * rows + first * 16 + (pos_a & 15)
    place_b = (pos_b >> 4) * rows + second * 16 + (pos_b & 15)
    slot = iota((rows, count), 0) + half * rows
    pick = jnp.where((slot == place_a) | (slot == place_b), 1.0, 0.0).astype(BF16)
    out_ref[...] = jnp.dot(pick, tok_ref[...], preferred_element_type=F32).astype(BF16)
    line = iota((128, count), 0)
    table = jnp.where(
        line == 0,
        place_a.astype(F32),
        jnp.where(
            line == 1,
            place_b.astype(F32),
            jnp.where(line == 2, gates_ref[0:1, :], jnp.where(line == 3, gates_ref[1:2, :], 0.0)),
        ),
    )
    col_ref[...] = table.T


def weights_kernel(sc, col_ref, high_ref, low_ref):
    slot = iota(high_ref.shape, 1)
    place_a = col_ref[:, 0:1].astype(jnp.int32)
    place_b = col_ref[:, 1:2].astype(jnp.int32)
    gate = jnp.where(slot == place_a, col_ref[:, 2:3], 0.0) + jnp.where(
        slot == place_b, col_ref[:, 3:4], 0.0
    )
    high = gate.astype(BF16)
    high_ref[...] = high
    low_ref[...] = (gate - high.astype(F32)).astype(BF16)


def product(rows, weights):
    return lax.dot_general(rows, weights, (((1,), (1,)), ((), ())), preferred_element_type=F32)


def joined_weights(refs, gate_w, up_w):
    own_gate, other_gate, own_up, other_up = refs
    part = own_gate.shape[0]
    gate_w[0:part, :] = own_gate[...]
    gate_w[part : 2 * part, :] = other_gate[...]
    up_w[0:part, :] = own_up[...]
    up_w[part : 2 * part, :] = other_up[...]


def first_kernel(sc, x0, x1, x2, w0, w1, w2, w3, gate_ref, up_ref, gate_w, up_w):
    width = x0.shape[1]
    for step, ref in enumerate((x0, x1, x2)):
        cols = pl.ds(pl.multiple_of(sc[3 + step] * width, width), width)
        joined_weights([w.at[:, cols] for w in (w0, w1, w2, w3)], gate_w, up_w)
        gate = product(ref[...], gate_w[...])
        up = product(ref[...], up_w[...])
        if step == 0:
            gate_ref[...] = gate
            up_ref[...] = up
        else:
            gate_ref[...] += gate
            up_ref[...] += up


def last_kernel(sc, top_ref, low_ref, w0, w1, w2, w3, gate_in, up_in, out_ref, gate_w, up_w):
    joined_weights((w0, w1, w2, w3), gate_w, up_w)
    middle = top_ref.shape[0]
    for ref, begin in ((top_ref, 0), (low_ref, middle)):
        rows = slice(begin, begin + middle)
        gate = gate_in[rows, :] + product(ref[...], gate_w[...])
        up = up_in[rows, :] + product(ref[...], up_w[...])
        out_ref[rows, :] = (gate / (1.0 + jnp.exp(-gate)) * up).astype(BF16)


def slab_kernel(sc, s0, s1, s2, s3, o0, o1, o2, o3):
    for ref, out in ((s0, o0), (s1, o1), (s2, o2), (s3, o3)):
        out[...] = ref[...]


def down_kernel(sc, h0, h1, h2, h3, *refs):
    near_ref, far_ref, out_ref, joined = refs
    part = near_ref.shape[1]
    share = out_ref.shape[2]
    for step in range(4):
        joined[step, 0:part, :] = near_ref[step]
        joined[step, part : 2 * part, :] = far_ref[step]
    for side in range(2):
        cols = slice(side * share, (side + 1) * share)
        total = jnp.dot(h0[...], joined[0, :, cols], preferred_element_type=F32)
        total += jnp.dot(h1[...], joined[1, :, cols], preferred_element_type=F32)
        total += jnp.dot(h2[...], joined[2, :, cols], preferred_element_type=F32)
        total += jnp.dot(h3[...], joined[3, :, cols], preferred_element_type=F32)
        out_ref[side] = total.astype(BF16)


def combine_kernel(sc, ret_ref, high_ref, low_ref, tok_ref, gain_ref, proj_ref, out_ref):
    mixed = jnp.dot(high_ref[...], ret_ref[...], preferred_element_type=F32)
    mixed += jnp.dot(low_ref[...], ret_ref[...], preferred_element_type=F32)
    feat = (tok_ref[...].astype(F32) + mixed).astype(BF16).astype(F32)
    square = jnp.sum(feat * feat, axis=1, keepdims=True)
    part = jnp.dot(
        (feat * gain_ref[...]).astype(BF16), proj_ref[...], preferred_element_type=F32
    )
    tiles, block, _ = out_ref.shape
    count, channels = part.shape
    lane = iota((count, 128), 1)
    high = square.astype(BF16).astype(F32)
    extra = jnp.where(lane == 0, high, jnp.where(lane == 1, square - high, 0.0))
    own = count // tiles
    border = (block - own) // 2
    for tile in range(tiles):
        begin = tile * own - border
        low, top = max(begin, 0), min(begin + block, count)
        for value, cols in (
            (part, slice(0, channels)),
            (extra, slice(channels, channels + 128)),
        ):
            pieces = [value[low:top, :]]
            if low > begin:
                pieces = [jnp.zeros((low - begin, value.shape[1]), F32)] + pieces
            if top < begin + block:
                pieces = pieces + [jnp.zeros((begin + block - top, value.shape[1]), F32)]
            joined = pieces[0] if len(pieces) == 1 else jnp.concatenate(pieces, axis=0)
            out_ref[tile, :, cols] = joined.astype(BF16)


def convolved(field, weights, rows):
    sums = []
    for col_step in range(3):
        total = None
        for row_step in range(3):
            term = jnp.dot(
                field[row_step * 16 : row_step * 16 + rows, :],
                weights(row_step, col_step),
                preferred_element_type=F32,
            )
            total = term if total is None else total + term
        sums.append(total)
    col = iota(sums[0].shape, 0) & 15
    left = jnp.where(col == 0, 0.0, pltpu.roll(sums[0], 1, 0))
    right = jnp.where(col == 15, 0.0, pltpu.roll(sums[2], rows - 1, 0))
    return sums[1] + left + right


def cache_kernel(sc, cache_ref, above_ref, below_ref, weight_ref, bias_ref, out_ref):
    head = sc[2]
    older = lax.rem(head + 2, 3)
    total = jnp.broadcast_to(bias_ref[...], out_ref.shape)
    for step, slot in ((0, older), (1, head)):
        field = jnp.concatenate([above_ref[slot], cache_ref[slot], below_ref[slot]], axis=0)
        total = total + convolved(field, lambda r, c: weight_ref[step, r, c], out_ref.shape[0])
    out_ref[...] = total


def tail_kernel(sc, arr_ref, past_ref, time_ref, space_ref, bias_ref, out_ref):
    tile = sc[0]
    total = arr_ref[0].astype(F32)
    for source in range(1, arr_ref.shape[0]):
        total = total + arr_ref[source].astype(F32)
    channels = out_ref.shape[1]
    square = total[:, channels : channels + 1] + total[:, channels + 1 : channels + 2]
    scale = lax.rsqrt(square / 4096.0 + EPS)
    coarse = (total[:, :channels] * scale).astype(BF16)
    block = coarse.shape[0]
    pixel = iota((4 * block, block), 0)
    spread = jnp.where(
        iota((4 * block, block), 1) == (pixel >> 5) * 8 + ((pixel & 15) >> 1), 1.0, 0.0
    ).astype(BF16)
    fine = jnp.dot(spread, coarse, preferred_element_type=F32)
    field = fine.astype(BF16)
    rows = past_ref.shape[0]
    first = past_ref[...] + convolved(field, lambda r, c: time_ref[0, r, c], rows)
    active = first / (1.0 + jnp.exp(-first))
    place = (iota(active.shape, 0) >> 4) + tile * 8 - 1
    active = jnp.where((place >= 0) & (place < 64), active, 0.0).astype(BF16)
    own = out_ref.shape[0]
    second = convolved(active, lambda r, c: space_ref[r, c], own)
    out_ref[...] = (fine[32 : 32 + own, :] + second + bias_ref[...]).astype(BF16)


def flipped(x, bits):
    return lax.ppermute(x, EXP, [(i, i ^ bits) for i in range(8)])


def swapped(x, axis):
    return lax.ppermute(x, axis, [(0, 1), (1, 0)])


def body(
    tokens,
    routes,
    gates,
    w_gate,
    w_up,
    w_down,
    feat_gain,
    w_proj,
    conv_time,
    bias_time,
    conv_space,
    bias_space,
    frame_cache,
    cache_head,
):
    tile = lax.axis_index(EXP).astype(jnp.int32)
    half = tile >> 2
    quarter = (tile & 3) ^ (half << 1)
    scalars = jnp.stack([tile, half, cache_head[0], quarter, quarter ^ 1, quarter ^ 2, quarter ^ 3])
    count, width = tokens.shape[1:]
    hid = w_gate.shape[2]
    channels = w_proj.shape[1]
    fourth = width // 4
    share = width // 8
    own_gate, own_up = w_gate[0].T, w_up[0].T

    with jax.named_scope("exchange_weights"):
        pairs = [(i, i ^ 6) for i in range(8)]
        other_gate = lax.ppermute(own_gate, EXP, pairs)
        later, other_gate = lax.optimization_barrier((own_up, other_gate))
        other_up = lax.ppermute(later, EXP, pairs)
        slabs = call(
            slab_kernel,
            "slabs",
            scalars,
            (w_down[0],) * 4,
            [pl.BlockSpec((hid, fourth), lambda i, s, k=k: (0, s[3 + k])) for k in range(4)],
            [jax.ShapeDtypeStruct((hid, fourth), BF16)] * 4,
        )
        near_2 = flipped(slabs[2], 2)
        near_1 = flipped(slabs[1], 1)
        near_3 = flipped(flipped(slabs[3], 1), 2)
        near = jnp.stack([slabs[0], near_2, near_1, near_3])

    with jax.named_scope("cache"):
        frames = frame_cache.reshape(3, 128, channels)
        above = lax.ppermute(frames[:, 96:], EXP, [(i, i + 1) for i in range(7)])
        below = lax.ppermute(frames[:, :32], EXP, [(i + 1, i) for i in range(7)])
        frames, other_gate = lax.optimization_barrier((frames, other_gate))
        past = call(
            cache_kernel,
            "cache",
            scalars,
            (frames, above, below, conv_time, bias_time.reshape(1, channels)),
            [
                whole(frames.shape),
                whole(above.shape),
                whole(below.shape),
                pl.BlockSpec((2, 3, 3, channels, channels), lambda i, s: (0, 0, 0, 0, 0)),
                whole((1, channels)),
            ],
            jax.ShapeDtypeStruct((160, channels), F32),
            cost=pl.CostEstimate(flops=8000 * 10**6, bytes_accessed=40 * 10**6, transcendentals=0),
        )

    with jax.named_scope("dispatch"):
        outgoing, columns = call(
            dispatch_kernel,
            "dispatch",
            scalars,
            (routes[0].T, gates[0].T, tokens[0]),
            [
                whole((2, count)),
                whole((2, count)),
                pl.BlockSpec((count, fourth), lambda i, s: (0, s[3])),
            ],
            [
                jax.ShapeDtypeStruct((512, fourth), BF16),
                jax.ShapeDtypeStruct((count, 128), F32),
            ],
        )
        arrived = lax.all_to_all(
            outgoing.reshape(32, 16, fourth), "sess", 0, 0, tiled=True
        ).reshape(512, fourth)
        high, low = call(
            weights_kernel,
            "weights",
            scalars,
            (columns,),
            [whole((count, 128))],
            [jax.ShapeDtypeStruct((count, 1024), BF16)] * 2,
        )

    with jax.named_scope("gather"):
        arrived, near, past, high, low = lax.optimization_barrier(
            (arrived, near, past, high, low)
        )
        from_y = swapped(arrived, "yl")
        from_x = swapped(arrived, "x")
        corner_top = swapped(from_y[:256], "x")
        corner_low = swapped(from_x[256:], "yl")
        arrived, from_x, from_y = lax.optimization_barrier((arrived, from_x, from_y))
        near, other_up = lax.optimization_barrier((near, other_up))
        far = flipped(near, 6)

    with jax.named_scope("experts"):
        weights = (own_gate, other_gate, own_up, other_up)
        pair = [jax.ShapeDtypeStruct((512, 2 * hid), F32)] * 2
        scratch = [pltpu.VMEM((2 * hid, fourth), BF16)] * 2
        acc = whole((512, 2 * hid))
        gate, up = call(
            first_kernel,
            "first",
            scalars,
            (arrived, from_x, from_y, *weights),
            [whole((512, fourth))] * 3 + [whole((hid, width))] * 4,
            pair,
            scratch,
            24,
        )
        hidden = call(
            last_kernel,
            "hidden",
            scalars,
            (corner_top, corner_low, *weights, gate, up),
            [whole((256, fourth))] * 2
            + [pl.BlockSpec((hid, fourth), lambda i, s: (0, s[6]))] * 4
            + [acc, acc],
            jax.ShapeDtypeStruct((512, 2 * hid), BF16),
            scratch,
            16,
        )

    with jax.named_scope("hidden_gather"):
        hidden_y = swapped(hidden, "yl")
        hidden_x = swapped(hidden, "x")
        hidden_c = lax.ppermute(hidden, ("yl", "x"), [(i, 3 - i) for i in range(4)])

    with jax.named_scope("down"):
        answer = call(
            down_kernel,
            "down",
            scalars,
            (hidden, hidden_y, hidden_x, hidden_c, near, far),
            [whole((512, 2 * hid))] * 4 + [whole((4, hid, fourth))] * 2,
            jax.ShapeDtypeStruct((2, 512, share), BF16),
            [pltpu.VMEM((4, 2 * hid, fourth), BF16)],
            20,
        )
        returned = lax.all_to_all(
            answer.reshape(64, 16, share),
            ("sess",) + EXP,
            0,
            0,
            axis_index_groups=[
                [s * 8 + 4 * h + (c ^ (2 * h)) for h in range(2) for s in range(32)]
                for c in range(4)
            ],
            tiled=True,
        ).reshape(1024, share)

    with jax.named_scope("combine"):
        blocks = call(
            combine_kernel,
            "combine",
            scalars,
            (returned, high, low, tokens[0], feat_gain.reshape(1, width), w_proj),
            [
                whole((1024, share)),
                whole((count, 1024)),
                whole((count, 1024)),
                pl.BlockSpec((count, share), lambda i, s: (0, s[3] * 2 + s[1])),
                pl.BlockSpec((1, share), lambda i, s: (0, s[3] * 2 + s[1])),
                pl.BlockSpec((share, channels), lambda i, s: (s[3] * 2 + s[1], 0)),
            ],
            jax.ShapeDtypeStruct((8, 48, channels + 128), BF16),
        )
        blocks = lax.all_to_all(blocks, EXP, 0, 0, tiled=True)

    with jax.named_scope("decode"):
        out = call(
            tail_kernel,
            "decode",
            scalars,
            (blocks, past, conv_time, conv_space, bias_space.reshape(1, channels)),
            [
                whole(blocks.shape),
                whole((160, channels)),
                pl.BlockSpec((1, 3, 3, channels, channels), lambda i, s: (2, 0, 0, 0, 0)),
                whole(conv_space.shape),
                whole((1, channels)),
            ],
            jax.ShapeDtypeStruct((128, channels), BF16),
        )
    return out.reshape(1, 8, 16, channels)


def solution(mesh):
    finer = Mesh(
        mesh.devices.reshape(mesh.shape["sess"], 2, 2, 2), ("sess", "yh", "yl", "x")
    )
    return jax.shard_map(
        body,
        mesh=finer,
        in_specs=(
            P("sess", None, None),
            P("sess", None, None),
            P("sess", None, None),
            P("sess", None, EXP),
            P("sess", None, EXP),
            P("sess", EXP, None),
            P(),
            P(),
            P(),
            P(),
            P(),
            P(),
            P(None, "sess", EXP, None, None),
            P("sess"),
        ),
        out_specs=P("sess", EXP, None, None),
        check_vma=False,
    )
```

```python
import jax
import jax.numpy as jnp
from jax import lax
from jax.experimental import pallas as pl
from jax.experimental.pallas import tpu as pltpu
from jax.sharding import Mesh
from jax.sharding import PartitionSpec as P

EXP = ("yh", "yl", "x")
EPS = 1e-06
F32 = jnp.float32
BF16 = jnp.bfloat16


def whole(shape):
    zeros = (0,) * len(shape)
    return pl.BlockSpec(shape, lambda i, s: zeros)


def call(kernel, name, scalars, operands, specs, outs, scratch=(), limit=12, cost=None):
    single = not isinstance(outs, (list, tuple))
    out_list = [outs] if single else list(outs)
    result = pl.pallas_call(
        kernel,
        name=name,
        out_shape=out_list,
        grid_spec=pltpu.PrefetchScalarGridSpec(
            num_scalar_prefetch=1,
            grid=(1,),
            in_specs=specs,
            out_specs=[whole(o.shape) for o in out_list],
            scratch_shapes=list(scratch),
        ),
        compiler_params=pltpu.CompilerParams(vmem_limit_bytes=limit * 1024 * 1024),
        cost_estimate=cost,
    )(scalars, *operands)
    return result[0] if single else result


def iota(shape, dim):
    return lax.broadcasted_iota(jnp.int32, shape, dim)


def dispatch_kernel(sc, routes_ref, gates_ref, tok_ref, out_ref, col_ref):
    half = sc[1]
    count = routes_ref.shape[1]
    rows = out_ref.shape[0]
    experts = iota((32, count), 0)
    first = routes_ref[0:1, :]
    second = routes_ref[1:2, :]
    is_first = experts == first
    is_second = experts == second
    named = jnp.where(is_first | is_second, 1.0, 0.0).astype(BF16)
    earlier = jnp.where(iota((count, count), 0) < iota((count, count), 1), 1.0, 0.0).astype(BF16)
    before = jnp.dot(named, earlier, preferred_element_type=F32)
    pos_a = jnp.sum(jnp.where(is_first, before, 0.0), axis=0, keepdims=True).astype(jnp.int32)
    pos_b = jnp.sum(jnp.where(is_second, before, 0.0), axis=0, keepdims=True).astype(jnp.int32)
    place_a = (pos_a >> 4) * rows + first * 16 + (pos_a & 15)
    place_b = (pos_b >> 4) * rows + second * 16 + (pos_b & 15)
    slot = iota((rows, count), 0) + half * rows
    pick = jnp.where((slot == place_a) | (slot == place_b), 1.0, 0.0).astype(BF16)
    out_ref[...] = jnp.dot(pick, tok_ref[...], preferred_element_type=F32).astype(BF16)
    line = iota((128, count), 0)
    table = jnp.where(
        line == 0,
        place_a.astype(F32),
        jnp.where(
            line == 1,
            place_b.astype(F32),
            jnp.where(line == 2, gates_ref[0:1, :], jnp.where(line == 3, gates_ref[1:2, :], 0.0)),
        ),
    )
    col_ref[...] = table.T


def weights_kernel(sc, col_ref, high_ref, low_ref):
    slot = iota(high_ref.shape, 1)
    place_a = col_ref[:, 0:1].astype(jnp.int32)
    place_b = col_ref[:, 1:2].astype(jnp.int32)
    gate = jnp.where(slot == place_a, col_ref[:, 2:3], 0.0) + jnp.where(
        slot == place_b, col_ref[:, 3:4], 0.0
    )
    high = gate.astype(BF16)
    high_ref[...] = high
    low_ref[...] = (gate - high.astype(F32)).astype(BF16)


def product(rows, weights):
    return lax.dot_general(rows, weights, (((1,), (1,)), ((), ())), preferred_element_type=F32)


def turned(hidden, weights):
    return lax.dot_general(hidden, weights, (((0,), (0,)), ((), ())), preferred_element_type=F32)


def joined_weights(refs, gate_w, up_w):
    own_gate, other_gate, own_up, other_up = refs
    part = own_gate.shape[0]
    gate_w[0:part, :] = own_gate[...]
    gate_w[part : 2 * part, :] = other_gate[...]
    up_w[0:part, :] = own_up[...]
    up_w[part : 2 * part, :] = other_up[...]


def first_kernel(sc, x0, x1, x2, w0, w1, w2, w3, gate_ref, up_ref, gate_w, up_w):
    width = x0.shape[1]
    for step, ref in enumerate((x0, x1, x2)):
        cols = pl.ds(pl.multiple_of(sc[3 + step] * width, width), width)
        joined_weights([w.at[:, cols] for w in (w0, w1, w2, w3)], gate_w, up_w)
        gate = product(gate_w[...], ref[...])
        up = product(up_w[...], ref[...])
        if step == 0:
            gate_ref[...] = gate
            up_ref[...] = up
        else:
            gate_ref[...] += gate
            up_ref[...] += up


def last_kernel(sc, top_ref, low_ref, w0, w1, w2, w3, gate_in, up_in, out_ref, gate_w, up_w):
    joined_weights((w0, w1, w2, w3), gate_w, up_w)
    middle = top_ref.shape[0]
    for ref, begin in ((top_ref, 0), (low_ref, middle)):
        rows = slice(begin, begin + middle)
        gate = gate_in[:, rows] + product(gate_w[...], ref[...])
        up = up_in[:, rows] + product(up_w[...], ref[...])
        out_ref[:, rows] = (gate / (1.0 + jnp.exp(-gate)) * up).astype(BF16)


def slab_kernel(sc, s0, s1, s2, s3, o0, o1, o2, o3):
    for ref, out in ((s0, o0), (s1, o1), (s2, o2), (s3, o3)):
        out[...] = ref[...]


def down_kernel(sc, h0, h1, h2, h3, *refs):
    near_ref, far_ref, out_ref, joined = refs
    part = near_ref.shape[1]
    share = out_ref.shape[2]
    for step in range(4):
        joined[step, 0:part, :] = near_ref[step]
        joined[step, part : 2 * part, :] = far_ref[step]
    for side in range(2):
        cols = slice(side * share, (side + 1) * share)
        total = turned(h0[...], joined[0, :, cols])
        total += turned(h1[...], joined[1, :, cols])
        total += turned(h2[...], joined[2, :, cols])
        total += turned(h3[...], joined[3, :, cols])
        out_ref[side] = total.astype(BF16)


def combine_kernel(sc, ret_ref, high_ref, low_ref, tok_ref, gain_ref, proj_ref, out_ref):
    mixed = jnp.dot(high_ref[...], ret_ref[...], preferred_element_type=F32)
    mixed += jnp.dot(low_ref[...], ret_ref[...], preferred_element_type=F32)
    feat = (tok_ref[...].astype(F32) + mixed).astype(BF16).astype(F32)
    square = jnp.sum(feat * feat, axis=1, keepdims=True)
    part = jnp.dot(
        (feat * gain_ref[...]).astype(BF16), proj_ref[...], preferred_element_type=F32
    )
    tiles, block, _ = out_ref.shape
    count, channels = part.shape
    lane = iota((count, 128), 1)
    high = square.astype(BF16).astype(F32)
    extra = jnp.where(lane == 0, high, jnp.where(lane == 1, square - high, 0.0))
    own = count // tiles
    border = (block - own) // 2
    for tile in range(tiles):
        begin = tile * own - border
        low, top = max(begin, 0), min(begin + block, count)
        for value, cols in (
            (part, slice(0, channels)),
            (extra, slice(channels, channels + 128)),
        ):
            pieces = [value[low:top, :]]
            if low > begin:
                pieces = [jnp.zeros((low - begin, value.shape[1]), F32)] + pieces
            if top < begin + block:
                pieces = pieces + [jnp.zeros((begin + block - top, value.shape[1]), F32)]
            joined = pieces[0] if len(pieces) == 1 else jnp.concatenate(pieces, axis=0)
            out_ref[tile, :, cols] = joined.astype(BF16)


def convolved(field, weights, rows):
    sums = []
    for col_step in range(3):
        total = None
        for row_step in range(3):
            term = jnp.dot(
                field[row_step * 16 : row_step * 16 + rows, :],
                weights(row_step, col_step),
                preferred_element_type=F32,
            )
            total = term if total is None else total + term
        sums.append(total)
    col = iota(sums[0].shape, 0) & 15
    left = jnp.where(col == 0, 0.0, pltpu.roll(sums[0], 1, 0))
    right = jnp.where(col == 15, 0.0, pltpu.roll(sums[2], rows - 1, 0))
    return sums[1] + left + right


def cache_kernel(sc, cache_ref, above_ref, below_ref, weight_ref, bias_ref, out_ref):
    head = sc[2]
    older = lax.rem(head + 2, 3)
    total = jnp.broadcast_to(bias_ref[...], out_ref.shape)
    for step, slot in ((0, older), (1, head)):
        field = jnp.concatenate([above_ref[slot], cache_ref[slot], below_ref[slot]], axis=0)
        total = total + convolved(field, lambda r, c: weight_ref[step, r, c], out_ref.shape[0])
    out_ref[...] = total


def tail_kernel(sc, arr_ref, past_ref, time_ref, space_ref, bias_ref, out_ref):
    tile = sc[0]
    total = arr_ref[0].astype(F32)
    for source in range(1, arr_ref.shape[0]):
        total = total + arr_ref[source].astype(F32)
    channels = out_ref.shape[1]
    square = total[:, channels : channels + 1] + total[:, channels + 1 : channels + 2]
    scale = lax.rsqrt(square / 4096.0 + EPS)
    coarse = (total[:, :channels] * scale).astype(BF16)
    block = coarse.shape[0]
    pixel = iota((4 * block, block), 0)
    spread = jnp.where(
        iota((4 * block, block), 1) == (pixel >> 5) * 8 + ((pixel & 15) >> 1), 1.0, 0.0
    ).astype(BF16)
    fine = jnp.dot(spread, coarse, preferred_element_type=F32)
    field = fine.astype(BF16)
    rows = past_ref.shape[0]
    first = past_ref[...] + convolved(field, lambda r, c: time_ref[0, r, c], rows)
    active = first / (1.0 + jnp.exp(-first))
    place = (iota(active.shape, 0) >> 4) + tile * 8 - 1
    active = jnp.where((place >= 0) & (place < 64), active, 0.0).astype(BF16)
    own = out_ref.shape[0]
    second = convolved(active, lambda r, c: space_ref[r, c], own)
    out_ref[...] = (fine[32 : 32 + own, :] + second + bias_ref[...]).astype(BF16)


def in_hbm(x):
    return pltpu.with_memory_space_constraint(x, pltpu.HBM)


def flipped(x, bits):
    return lax.ppermute(x, EXP, [(i, i ^ bits) for i in range(8)])


def swapped(x, axis):
    return lax.ppermute(x, axis, [(0, 1), (1, 0)])


def body(
    tokens,
    routes,
    gates,
    w_gate,
    w_up,
    w_down,
    feat_gain,
    w_proj,
    conv_time,
    bias_time,
    conv_space,
    bias_space,
    frame_cache,
    cache_head,
):
    tile = lax.axis_index(EXP).astype(jnp.int32)
    half = tile >> 2
    quarter = (tile & 3) ^ (half << 1)
    scalars = jnp.stack([tile, half, cache_head[0], quarter, quarter ^ 1, quarter ^ 2, quarter ^ 3])
    count, width = tokens.shape[1:]
    hid = w_gate.shape[2]
    channels = w_proj.shape[1]
    fourth = width // 4
    share = width // 8
    own_gate, own_up = w_gate[0].T, w_up[0].T

    with jax.named_scope("exchange_weights"):
        pairs = [(i, i ^ 6) for i in range(8)]
        other_gate = lax.ppermute(own_gate, EXP, pairs)
        slabs = call(
            slab_kernel,
            "slabs",
            scalars,
            (w_down[0],) * 4,
            [pl.BlockSpec((hid, fourth), lambda i, s, k=k: (0, s[3 + k])) for k in range(4)],
            [jax.ShapeDtypeStruct((hid, fourth), BF16)] * 4,
        )
        near_1, near_2, near_3 = [flipped(slabs[k], k) for k in (1, 2, 3)]
        later, other_gate = lax.optimization_barrier((own_up, other_gate))
        other_up = lax.ppermute(later, EXP, pairs)

    with jax.named_scope("cache"):
        frames = frame_cache.reshape(3, 128, channels)
        above = lax.ppermute(frames[:, 96:], EXP, [(i, i + 1) for i in range(7)])
        below = lax.ppermute(frames[:, :32], EXP, [(i + 1, i) for i in range(7)])
        frames, *_ = lax.optimization_barrier((frames, near_1, near_2, near_3))
        past = call(
            cache_kernel,
            "cache",
            scalars,
            (
                in_hbm(frames),
                above,
                below,
                in_hbm(conv_time),
                in_hbm(bias_time.reshape(1, channels)),
            ),
            [
                whole(frames.shape),
                whole(above.shape),
                whole(below.shape),
                pl.BlockSpec((2, 3, 3, channels, channels), lambda i, s: (0, 0, 0, 0, 0)),
                whole((1, channels)),
            ],
            jax.ShapeDtypeStruct((160, channels), F32),
            cost=pl.CostEstimate(flops=16000 * 10**6, bytes_accessed=80 * 10**6, transcendentals=0),
        )

    with jax.named_scope("dispatch"):
        outgoing, columns = call(
            dispatch_kernel,
            "dispatch",
            scalars,
            (in_hbm(routes[0].T), in_hbm(gates[0].T), in_hbm(tokens[0])),
            [
                whole((2, count)),
                whole((2, count)),
                pl.BlockSpec((count, fourth), lambda i, s: (0, s[3])),
            ],
            [
                jax.ShapeDtypeStruct((512, fourth), BF16),
                jax.ShapeDtypeStruct((count, 128), F32),
            ],
        )
        arrived = lax.all_to_all(
            outgoing.reshape(32, 16, fourth), "sess", 0, 0, tiled=True
        ).reshape(512, fourth)
        columns, _ = lax.optimization_barrier((columns, other_gate))
        high, low = call(
            weights_kernel,
            "weights",
            scalars,
            (columns,),
            [whole((count, 128))],
            [jax.ShapeDtypeStruct((count, 1024), BF16)] * 2,
            cost=pl.CostEstimate(flops=12000 * 10**6, bytes_accessed=60 * 10**6, transcendentals=0),
        )

    with jax.named_scope("gather"):
        arrived, near_1, near_2, near_3, high, low = lax.optimization_barrier(
            (arrived, near_1, near_2, near_3, high, low)
        )
        near = jnp.stack([slabs[0], near_2, near_1, near_3])
        from_y = swapped(arrived, "yl")
        from_x = swapped(arrived, "x")
        from_x, from_y, past = lax.optimization_barrier((from_x, from_y, past))
        corner_top = swapped(from_y[:256], "x")
        corner_low = swapped(from_x[256:], "yl")
        arrived, from_x, from_y = lax.optimization_barrier((arrived, from_x, from_y))
        near, other_up = lax.optimization_barrier((near, other_up))
        far = flipped(near, 6)

    with jax.named_scope("experts"):
        weights = (own_gate, other_gate, own_up, other_up)
        pair = [jax.ShapeDtypeStruct((2 * hid, 512), F32)] * 2
        scratch = [pltpu.VMEM((2 * hid, fourth), BF16)] * 2
        acc = whole((2 * hid, 512))
        gate, up = call(
            first_kernel,
            "first",
            scalars,
            (arrived, from_x, from_y, *weights),
            [whole((512, fourth))] * 3 + [whole((hid, width))] * 4,
            pair,
            scratch,
            24,
        )
        hidden = call(
            last_kernel,
            "hidden",
            scalars,
            (corner_top, corner_low, *weights, gate, up),
            [whole((256, fourth))] * 2
            + [pl.BlockSpec((hid, fourth), lambda i, s: (0, s[6]))] * 4
            + [acc, acc],
            jax.ShapeDtypeStruct((2 * hid, 512), BF16),
            scratch,
            16,
        )

    with jax.named_scope("hidden_gather"):
        hidden_y = swapped(hidden, "yl")
        hidden_x = swapped(hidden, "x")
        hidden_c = lax.ppermute(hidden, ("yl", "x"), [(i, 3 - i) for i in range(4)])

    with jax.named_scope("down"):
        answer = call(
            down_kernel,
            "down",
            scalars,
            (hidden, hidden_y, hidden_x, hidden_c, near, far),
            [whole((2 * hid, 512))] * 4 + [whole((4, hid, fourth))] * 2,
            jax.ShapeDtypeStruct((2, 512, share), BF16),
            [pltpu.VMEM((4, 2 * hid, fourth), BF16)],
            20,
        )
        returned = lax.all_to_all(
            answer.reshape(64, 16, share),
            ("sess",) + EXP,
            0,
            0,
            axis_index_groups=[
                [s * 8 + 4 * h + (c ^ (2 * h)) for h in range(2) for s in range(32)]
                for c in range(4)
            ],
            tiled=True,
        ).reshape(1024, share)

    with jax.named_scope("combine"):
        blocks = call(
            combine_kernel,
            "combine",
            scalars,
            (returned, high, low, tokens[0], feat_gain.reshape(1, width), w_proj),
            [
                whole((1024, share)),
                whole((count, 1024)),
                whole((count, 1024)),
                pl.BlockSpec((count, share), lambda i, s: (0, s[3] * 2 + s[1])),
                pl.BlockSpec((1, share), lambda i, s: (0, s[3] * 2 + s[1])),
                pl.BlockSpec((share, channels), lambda i, s: (s[3] * 2 + s[1], 0)),
            ],
            jax.ShapeDtypeStruct((8, 48, channels + 128), BF16),
        )
        blocks = lax.all_to_all(blocks, EXP, 0, 0, tiled=True)

    with jax.named_scope("decode"):
        out = call(
            tail_kernel,
            "decode",
            scalars,
            (blocks, past, conv_time, conv_space, bias_space.reshape(1, channels)),
            [
                whole(blocks.shape),
                whole((160, channels)),
                pl.BlockSpec((1, 3, 3, channels, channels), lambda i, s: (2, 0, 0, 0, 0)),
                whole(conv_space.shape),
                whole((1, channels)),
            ],
            jax.ShapeDtypeStruct((128, channels), BF16),
        )
    return out.reshape(1, 8, 16, channels)


def solution(mesh):
    finer = Mesh(
        mesh.devices.reshape(mesh.shape["sess"], 2, 2, 2), ("sess", "yh", "yl", "x")
    )
    return jax.shard_map(
        body,
        mesh=finer,
        in_specs=(
            P("sess", None, None),
            P("sess", None, None),
            P("sess", None, None),
            P("sess", None, EXP),
            P("sess", None, EXP),
            P("sess", EXP, None),
            P(),
            P(),
            P(),
            P(),
            P(),
            P(),
            P(None, "sess", EXP, None, None),
            P("sess"),
        ),
        out_specs=P("sess", EXP, None, None),
        check_vma=False,
    )
```

```python
import jax
import jax.numpy as jnp
from jax import lax
from jax.experimental import pallas as pl
from jax.experimental.pallas import tpu as pltpu
from jax.sharding import Mesh
from jax.sharding import PartitionSpec as P

EXP = ("yh", "yl", "x")
EPS = 1e-06
F32 = jnp.float32
BF16 = jnp.bfloat16


def whole(shape):
    zeros = (0,) * len(shape)
    return pl.BlockSpec(shape, lambda i, s: zeros)


def call(kernel, name, scalars, operands, specs, outs, scratch=(), limit=12, cost=None):
    single = not isinstance(outs, (list, tuple))
    out_list = [outs] if single else list(outs)
    result = pl.pallas_call(
        kernel,
        name=name,
        out_shape=out_list,
        grid_spec=pltpu.PrefetchScalarGridSpec(
            num_scalar_prefetch=1,
            grid=(1,),
            in_specs=specs,
            out_specs=[whole(o.shape) for o in out_list],
            scratch_shapes=list(scratch),
        ),
        compiler_params=pltpu.CompilerParams(vmem_limit_bytes=limit * 1024 * 1024),
        cost_estimate=cost,
    )(scalars, *operands)
    return result[0] if single else result


def iota(shape, dim):
    return lax.broadcasted_iota(jnp.int32, shape, dim)


def dispatch_kernel(sc, routes_ref, gates_ref, tok_ref, out_ref, col_ref):
    half = sc[1]
    count = routes_ref.shape[1]
    rows = out_ref.shape[0]
    experts = iota((32, count), 0)
    first = routes_ref[0:1, :]
    second = routes_ref[1:2, :]
    is_first = experts == first
    is_second = experts == second
    named = jnp.where(is_first | is_second, 1.0, 0.0).astype(BF16)
    earlier = jnp.where(iota((count, count), 0) < iota((count, count), 1), 1.0, 0.0).astype(BF16)
    before = jnp.dot(named, earlier, preferred_element_type=F32)
    pos_a = jnp.sum(jnp.where(is_first, before, 0.0), axis=0, keepdims=True).astype(jnp.int32)
    pos_b = jnp.sum(jnp.where(is_second, before, 0.0), axis=0, keepdims=True).astype(jnp.int32)
    place_a = (pos_a >> 4) * rows + first * 16 + (pos_a & 15)
    place_b = (pos_b >> 4) * rows + second * 16 + (pos_b & 15)
    slot = iota((rows, count), 0) + half * rows
    pick = jnp.where((slot == place_a) | (slot == place_b), 1.0, 0.0).astype(BF16)
    out_ref[...] = jnp.dot(pick, tok_ref[...], preferred_element_type=F32).astype(BF16)
    line = iota((128, count), 0)
    table = jnp.where(
        line == 0,
        place_a.astype(F32),
        jnp.where(
            line == 1,
            place_b.astype(F32),
            jnp.where(line == 2, gates_ref[0:1, :], jnp.where(line == 3, gates_ref[1:2, :], 0.0)),
        ),
    )
    col_ref[...] = table.T


def weights_kernel(sc, col_ref, high_ref, low_ref):
    slot = iota(high_ref.shape, 1)
    place_a = col_ref[:, 0:1].astype(jnp.int32)
    place_b = col_ref[:, 1:2].astype(jnp.int32)
    gate = jnp.where(slot == place_a, col_ref[:, 2:3], 0.0) + jnp.where(
        slot == place_b, col_ref[:, 3:4], 0.0
    )
    high = gate.astype(BF16)
    high_ref[...] = high
    low_ref[...] = (gate - high.astype(F32)).astype(BF16)


def product(rows, weights):
    return lax.dot_general(rows, weights, (((1,), (1,)), ((), ())), preferred_element_type=F32)


def turned(hidden, weights):
    return lax.dot_general(hidden, weights, (((0,), (0,)), ((), ())), preferred_element_type=F32)


def joined_weights(refs, gate_w, up_w):
    own_gate, other_gate, own_up, other_up = refs
    part = own_gate.shape[0]
    gate_w[0:part, :] = own_gate[...]
    gate_w[part : 2 * part, :] = other_gate[...]
    up_w[0:part, :] = own_up[...]
    up_w[part : 2 * part, :] = other_up[...]


def first_kernel(sc, x0, x1, x2, w0, w1, w2, w3, gate_ref, up_ref, gate_w, up_w):
    width = x0.shape[1]
    for step, ref in enumerate((x0, x1, x2)):
        cols = pl.ds(pl.multiple_of(sc[3 + step] * width, width), width)
        joined_weights([w.at[:, cols] for w in (w0, w1, w2, w3)], gate_w, up_w)
        gate = product(gate_w[...], ref[...])
        up = product(up_w[...], ref[...])
        if step == 0:
            gate_ref[...] = gate
            up_ref[...] = up
        else:
            gate_ref[...] += gate
            up_ref[...] += up


def last_kernel(sc, top_ref, low_ref, w0, w1, w2, w3, gate_in, up_in, out_ref, gate_w, up_w):
    joined_weights((w0, w1, w2, w3), gate_w, up_w)
    middle = top_ref.shape[0]
    for ref, begin in ((top_ref, 0), (low_ref, middle)):
        rows = slice(begin, begin + middle)
        gate = gate_in[:, rows] + product(gate_w[...], ref[...])
        up = up_in[:, rows] + product(up_w[...], ref[...])
        out_ref[:, rows] = (gate / (1.0 + jnp.exp(-gate)) * up).astype(BF16)


def slab_kernel(sc, s0, s1, s2, s3, o0, o1, o2, o3):
    for ref, out in ((s0, o0), (s1, o1), (s2, o2), (s3, o3)):
        out[...] = ref[...]


def down_kernel(sc, h0, h1, h2, h3, *refs):
    near_ref, far_ref, out_ref = refs
    part = near_ref.shape[1]
    share = out_ref.shape[2]
    for side in range(2):
        cols = slice(side * share, (side + 1) * share)
        total = turned(h0[0:part, :], near_ref[0, :, cols])
        for step, ref in enumerate((h0, h1, h2, h3)):
            if step:
                total += turned(ref[0:part, :], near_ref[step, :, cols])
            total += turned(ref[part : 2 * part, :], far_ref[step, :, cols])
        out_ref[side] = total.astype(BF16)


def combine_kernel(sc, ret_ref, high_ref, low_ref, tok_ref, gain_ref, proj_ref, out_ref):
    mixed = jnp.dot(high_ref[...], ret_ref[...], preferred_element_type=F32)
    mixed += jnp.dot(low_ref[...], ret_ref[...], preferred_element_type=F32)
    feat = (tok_ref[...].astype(F32) + mixed).astype(BF16).astype(F32)
    square = jnp.sum(feat * feat, axis=1, keepdims=True)
    part = jnp.dot(
        (feat * gain_ref[...]).astype(BF16), proj_ref[...], preferred_element_type=F32
    )
    tiles, block, _ = out_ref.shape
    count, channels = part.shape
    lane = iota((count, 128), 1)
    high = square.astype(BF16).astype(F32)
    extra = jnp.where(lane == 0, high, jnp.where(lane == 1, square - high, 0.0))
    own = count // tiles
    border = (block - own) // 2
    for tile in range(tiles):
        begin = tile * own - border
        low, top = max(begin, 0), min(begin + block, count)
        for value, cols in (
            (part, slice(0, channels)),
            (extra, slice(channels, channels + 128)),
        ):
            pieces = [value[low:top, :]]
            if low > begin:
                pieces = [jnp.zeros((low - begin, value.shape[1]), F32)] + pieces
            if top < begin + block:
                pieces = pieces + [jnp.zeros((begin + block - top, value.shape[1]), F32)]
            joined = pieces[0] if len(pieces) == 1 else jnp.concatenate(pieces, axis=0)
            out_ref[tile, :, cols] = joined.astype(BF16)


def convolved(field, weights, rows):
    sums = []
    for col_step in range(3):
        total = None
        for row_step in range(3):
            term = jnp.dot(
                field[row_step * 16 : row_step * 16 + rows, :],
                weights(row_step, col_step),
                preferred_element_type=F32,
            )
            total = term if total is None else total + term
        sums.append(total)
    col = iota(sums[0].shape, 0) & 15
    left = jnp.where(col == 0, 0.0, pltpu.roll(sums[0], 1, 0))
    right = jnp.where(col == 15, 0.0, pltpu.roll(sums[2], rows - 1, 0))
    return sums[1] + left + right


def cache_kernel(sc, cache_ref, above_ref, below_ref, weight_ref, bias_ref, out_ref):
    head = sc[2]
    older = lax.rem(head + 2, 3)
    total = jnp.broadcast_to(bias_ref[...], out_ref.shape)
    for step, slot in ((0, older), (1, head)):
        field = jnp.concatenate([above_ref[slot], cache_ref[slot], below_ref[slot]], axis=0)
        total = total + convolved(field, lambda r, c: weight_ref[step, r, c], out_ref.shape[0])
    out_ref[...] = total


def tail_kernel(sc, arr_ref, past_ref, time_ref, space_ref, bias_ref, out_ref):
    tile = sc[0]
    total = arr_ref[0].astype(F32)
    for source in range(1, arr_ref.shape[0]):
        total = total + arr_ref[source].astype(F32)
    channels = out_ref.shape[1]
    square = total[:, channels : channels + 1] + total[:, channels + 1 : channels + 2]
    scale = lax.rsqrt(square / 4096.0 + EPS)
    coarse = (total[:, :channels] * scale).astype(BF16)
    block = coarse.shape[0]
    pixel = iota((4 * block, block), 0)
    spread = jnp.where(
        iota((4 * block, block), 1) == (pixel >> 5) * 8 + ((pixel & 15) >> 1), 1.0, 0.0
    ).astype(BF16)
    fine = jnp.dot(spread, coarse, preferred_element_type=F32)
    field = fine.astype(BF16)
    rows = past_ref.shape[0]
    first = past_ref[...] + convolved(field, lambda r, c: time_ref[0, r, c], rows)
    active = first / (1.0 + jnp.exp(-first))
    place = (iota(active.shape, 0) >> 4) + tile * 8 - 1
    active = jnp.where((place >= 0) & (place < 64), active, 0.0).astype(BF16)
    own = out_ref.shape[0]
    second = convolved(active, lambda r, c: space_ref[r, c], own)
    out_ref[...] = (fine[32 : 32 + own, :] + second + bias_ref[...]).astype(BF16)


def in_hbm(x):
    return pltpu.with_memory_space_constraint(x, pltpu.HBM)


def flipped(x, bits):
    return lax.ppermute(x, EXP, [(i, i ^ bits) for i in range(8)])


def swapped(x, axis):
    return lax.ppermute(x, axis, [(0, 1), (1, 0)])


def body(
    tokens,
    routes,
    gates,
    w_gate,
    w_up,
    w_down,
    feat_gain,
    w_proj,
    conv_time,
    bias_time,
    conv_space,
    bias_space,
    frame_cache,
    cache_head,
):
    tile = lax.axis_index(EXP).astype(jnp.int32)
    half = tile >> 2
    quarter = (tile & 3) ^ (half << 1)
    scalars = jnp.stack([tile, half, cache_head[0], quarter, quarter ^ 1, quarter ^ 2, quarter ^ 3])
    count, width = tokens.shape[1:]
    hid = w_gate.shape[2]
    channels = w_proj.shape[1]
    fourth = width // 4
    share = width // 8
    own_gate, own_up = w_gate[0].T, w_up[0].T

    with jax.named_scope("exchange_weights"):
        pairs = [(i, i ^ 6) for i in range(8)]
        other_gate = lax.ppermute(own_gate, EXP, pairs)
        slabs = call(
            slab_kernel,
            "slabs",
            scalars,
            (w_down[0],) * 4,
            [pl.BlockSpec((hid, fourth), lambda i, s, k=k: (0, s[3 + k])) for k in range(4)],
            [jax.ShapeDtypeStruct((hid, fourth), BF16)] * 4,
        )
        near_1, near_2, near_3 = [flipped(slabs[k], k) for k in (1, 2, 3)]
        later, other_gate = lax.optimization_barrier((own_up, other_gate))
        other_up = lax.ppermute(later, EXP, pairs)

    with jax.named_scope("cache"):
        frames = frame_cache.reshape(3, 128, channels)
        above = lax.ppermute(frames[:, 96:], EXP, [(i, i + 1) for i in range(7)])
        below = lax.ppermute(frames[:, :32], EXP, [(i + 1, i) for i in range(7)])
        frames, *_ = lax.optimization_barrier((frames, near_1, near_2, near_3))
        past = call(
            cache_kernel,
            "cache",
            scalars,
            (
                in_hbm(frames),
                above,
                below,
                in_hbm(conv_time),
                in_hbm(bias_time.reshape(1, channels)),
            ),
            [
                whole(frames.shape),
                whole(above.shape),
                whole(below.shape),
                pl.BlockSpec((2, 3, 3, channels, channels), lambda i, s: (0, 0, 0, 0, 0)),
                whole((1, channels)),
            ],
            jax.ShapeDtypeStruct((160, channels), F32),
            cost=pl.CostEstimate(flops=16000 * 10**6, bytes_accessed=80 * 10**6, transcendentals=0),
        )

    with jax.named_scope("dispatch"):
        outgoing, columns = call(
            dispatch_kernel,
            "dispatch",
            scalars,
            (in_hbm(routes[0].T), in_hbm(gates[0].T), in_hbm(tokens[0])),
            [
                whole((2, count)),
                whole((2, count)),
                pl.BlockSpec((count, fourth), lambda i, s: (0, s[3])),
            ],
            [
                jax.ShapeDtypeStruct((512, fourth), BF16),
                jax.ShapeDtypeStruct((count, 128), F32),
            ],
        )
        arrived = lax.all_to_all(
            outgoing.reshape(32, 16, fourth), "sess", 0, 0, tiled=True
        ).reshape(512, fourth)
        columns, _ = lax.optimization_barrier((columns, other_gate))
        high, low = call(
            weights_kernel,
            "weights",
            scalars,
            (columns,),
            [whole((count, 128))],
            [jax.ShapeDtypeStruct((count, 1024), BF16)] * 2,
            cost=pl.CostEstimate(flops=12000 * 10**6, bytes_accessed=60 * 10**6, transcendentals=0),
        )

    with jax.named_scope("gather"):
        arrived, near_1, near_2, near_3, high, low = lax.optimization_barrier(
            (arrived, near_1, near_2, near_3, high, low)
        )
        near = jnp.stack([slabs[0], near_2, near_1, near_3])
        from_y = swapped(arrived, "yl")
        from_x = swapped(arrived, "x")
        from_x, from_y, past = lax.optimization_barrier((from_x, from_y, past))
        corner_top = swapped(from_y[:256], "x")
        corner_low = swapped(from_x[256:], "yl")
        arrived, from_x, from_y = lax.optimization_barrier((arrived, from_x, from_y))
        near, other_up = lax.optimization_barrier((near, other_up))
        far = flipped(near, 6)

    with jax.named_scope("experts"):
        weights = (own_gate, other_gate, own_up, other_up)
        pair = [jax.ShapeDtypeStruct((2 * hid, 512), F32)] * 2
        scratch = [pltpu.VMEM((2 * hid, fourth), BF16)] * 2
        acc = whole((2 * hid, 512))
        gate, up = call(
            first_kernel,
            "first",
            scalars,
            (arrived, from_x, from_y, *weights),
            [whole((512, fourth))] * 3 + [whole((hid, width))] * 4,
            pair,
            scratch,
            24,
        )
        hidden = call(
            last_kernel,
            "hidden",
            scalars,
            (corner_top, corner_low, *weights, gate, up),
            [whole((256, fourth))] * 2
            + [pl.BlockSpec((hid, fourth), lambda i, s: (0, s[6]))] * 4
            + [acc, acc],
            jax.ShapeDtypeStruct((2 * hid, 512), BF16),
            scratch,
            16,
        )

    with jax.named_scope("hidden_gather"):
        hidden_y = swapped(hidden, "yl")
        hidden_x = swapped(hidden, "x")
        hidden_c = lax.ppermute(hidden, ("yl", "x"), [(i, 3 - i) for i in range(4)])

    with jax.named_scope("down"):
        answer = call(
            down_kernel,
            "down",
            scalars,
            (hidden, hidden_y, hidden_x, hidden_c, near, far),
            [whole((2 * hid, 512))] * 4 + [whole((4, hid, fourth))] * 2,
            jax.ShapeDtypeStruct((2, 512, share), BF16),
            [],
            20,
        )
        returned = lax.all_to_all(
            answer.reshape(64, 16, share),
            ("sess",) + EXP,
            0,
            0,
            axis_index_groups=[
                [s * 8 + 4 * h + (c ^ (2 * h)) for h in range(2) for s in range(32)]
                for c in range(4)
            ],
            tiled=True,
        ).reshape(1024, share)

    with jax.named_scope("combine"):
        blocks = call(
            combine_kernel,
            "combine",
            scalars,
            (returned, high, low, tokens[0], feat_gain.reshape(1, width), w_proj),
            [
                whole((1024, share)),
                whole((count, 1024)),
                whole((count, 1024)),
                pl.BlockSpec((count, share), lambda i, s: (0, s[3] * 2 + s[1])),
                pl.BlockSpec((1, share), lambda i, s: (0, s[3] * 2 + s[1])),
                pl.BlockSpec((share, channels), lambda i, s: (s[3] * 2 + s[1], 0)),
            ],
            jax.ShapeDtypeStruct((8, 48, channels + 128), BF16),
        )
        blocks = lax.all_to_all(blocks, EXP, 0, 0, tiled=True)

    with jax.named_scope("decode"):
        out = call(
            tail_kernel,
            "decode",
            scalars,
            (blocks, past, conv_time, conv_space, bias_space.reshape(1, channels)),
            [
                whole(blocks.shape),
                whole((160, channels)),
                pl.BlockSpec((1, 3, 3, channels, channels), lambda i, s: (2, 0, 0, 0, 0)),
                whole(conv_space.shape),
                whole((1, channels)),
            ],
            jax.ShapeDtypeStruct((128, channels), BF16),
        )
    return out.reshape(1, 8, 16, channels)


def solution(mesh):
    finer = Mesh(
        mesh.devices.reshape(mesh.shape["sess"], 2, 2, 2), ("sess", "yh", "yl", "x")
    )
    return jax.shard_map(
        body,
        mesh=finer,
        in_specs=(
            P("sess", None, None),
            P("sess", None, None),
            P("sess", None, None),
            P("sess", None, EXP),
            P("sess", None, EXP),
            P("sess", EXP, None),
            P(),
            P(),
            P(),
            P(),
            P(),
            P(),
            P(None, "sess", EXP, None, None),
            P("sess"),
        ),
        out_specs=P("sess", EXP, None, None),
        check_vma=False,
    )
```

```python
import jax
import jax.numpy as jnp
from jax import lax
from jax.experimental import pallas as pl
from jax.experimental.pallas import tpu as pltpu
from jax.sharding import Mesh
from jax.sharding import PartitionSpec as P

EXP = ("yh", "yl", "x")
EPS = 1e-06
F32 = jnp.float32
BF16 = jnp.bfloat16


def whole(shape):
    zeros = (0,) * len(shape)
    return pl.BlockSpec(shape, lambda i, s: zeros)


def call(kernel, name, scalars, operands, specs, outs, scratch=(), limit=12, cost=None):
    single = not isinstance(outs, (list, tuple))
    out_list = [outs] if single else list(outs)
    result = pl.pallas_call(
        kernel,
        name=name,
        out_shape=out_list,
        grid_spec=pltpu.PrefetchScalarGridSpec(
            num_scalar_prefetch=1,
            grid=(1,),
            in_specs=specs,
            out_specs=[whole(o.shape) for o in out_list],
            scratch_shapes=list(scratch),
        ),
        compiler_params=pltpu.CompilerParams(vmem_limit_bytes=limit * 1024 * 1024),
        cost_estimate=cost,
    )(scalars, *operands)
    return result[0] if single else result


def iota(shape, dim):
    return lax.broadcasted_iota(jnp.int32, shape, dim)


def places_of(routes_ref, rows):
    count = routes_ref.shape[1]
    experts = iota((32, count), 0)
    first = routes_ref[0:1, :]
    second = routes_ref[1:2, :]
    is_first = experts == first
    is_second = experts == second
    named = jnp.where(is_first | is_second, 1.0, 0.0).astype(BF16)
    earlier = jnp.where(iota((count, count), 0) < iota((count, count), 1), 1.0, 0.0).astype(BF16)
    before = jnp.dot(named, earlier, preferred_element_type=F32)
    pos_a = jnp.sum(jnp.where(is_first, before, 0.0), axis=0, keepdims=True).astype(jnp.int32)
    pos_b = jnp.sum(jnp.where(is_second, before, 0.0), axis=0, keepdims=True).astype(jnp.int32)
    place_a = (pos_a >> 4) * rows + first * 16 + (pos_a & 15)
    place_b = (pos_b >> 4) * rows + second * 16 + (pos_b & 15)
    return place_a, place_b


def dispatch_kernel(sc, routes_ref, tok_ref, out_ref):
    half = sc[1]
    count = routes_ref.shape[1]
    rows = out_ref.shape[0]
    place_a, place_b = places_of(routes_ref, rows)
    slot = iota((rows, count), 0) + half * rows
    pick = jnp.where((slot == place_a) | (slot == place_b), 1.0, 0.0).astype(BF16)
    out_ref[...] = jnp.dot(pick, tok_ref[...], preferred_element_type=F32).astype(BF16)


def columns_kernel(sc, routes_ref, gates_ref, col_ref):
    count = routes_ref.shape[1]
    place_a, place_b = places_of(routes_ref, 512)
    line = iota((128, count), 0)
    table = jnp.where(
        line == 0,
        place_a.astype(F32),
        jnp.where(
            line == 1,
            place_b.astype(F32),
            jnp.where(line == 2, gates_ref[0:1, :], jnp.where(line == 3, gates_ref[1:2, :], 0.0)),
        ),
    )
    col_ref[...] = table.T


def weights_kernel(sc, col_ref, high_ref, low_ref):
    slot = iota(high_ref.shape, 1)
    place_a = col_ref[:, 0:1].astype(jnp.int32)
    place_b = col_ref[:, 1:2].astype(jnp.int32)
    gate = jnp.where(slot == place_a, col_ref[:, 2:3], 0.0) + jnp.where(
        slot == place_b, col_ref[:, 3:4], 0.0
    )
    high = gate.astype(BF16)
    high_ref[...] = high
    low_ref[...] = (gate - high.astype(F32)).astype(BF16)


def product(rows, weights):
    return lax.dot_general(rows, weights, (((1,), (1,)), ((), ())), preferred_element_type=F32)


def turned(hidden, weights):
    return lax.dot_general(hidden, weights, (((0,), (0,)), ((), ())), preferred_element_type=F32)


def joined_weights(refs, gate_w, up_w):
    own_gate, other_gate, own_up, other_up = refs
    part = own_gate.shape[0]
    gate_w[0:part, :] = own_gate[...]
    gate_w[part : 2 * part, :] = other_gate[...]
    up_w[0:part, :] = own_up[...]
    up_w[part : 2 * part, :] = other_up[...]


def first_kernel(sc, x0, x1, x2, w0, w1, w2, w3, gate_ref, up_ref, gate_w, up_w):
    width = x0.shape[1]
    for step, ref in enumerate((x0, x1, x2)):
        cols = pl.ds(pl.multiple_of(sc[3 + step] * width, width), width)
        joined_weights([w.at[:, cols] for w in (w0, w1, w2, w3)], gate_w, up_w)
        gate = product(gate_w[...], ref[...])
        up = product(up_w[...], ref[...])
        if step == 0:
            gate_ref[...] = gate
            up_ref[...] = up
        else:
            gate_ref[...] += gate
            up_ref[...] += up


def last_kernel(sc, top_ref, low_ref, w0, w1, w2, w3, gate_in, up_in, out_ref, gate_w, up_w):
    joined_weights((w0, w1, w2, w3), gate_w, up_w)
    middle = top_ref.shape[0]
    for ref, begin in ((top_ref, 0), (low_ref, middle)):
        rows = slice(begin, begin + middle)
        gate = gate_in[:, rows] + product(gate_w[...], ref[...])
        up = up_in[:, rows] + product(up_w[...], ref[...])
        out_ref[:, rows] = (gate / (1.0 + jnp.exp(-gate)) * up).astype(BF16)


def slab_kernel(sc, s0, s1, s2, s3, o0, o1, o2, o3):
    for ref, out in ((s0, o0), (s1, o1), (s2, o2), (s3, o3)):
        out[...] = ref[...]


def down_kernel(sc, h0, h1, h2, h3, *refs):
    near_ref, far_ref, out_ref = refs
    part = near_ref.shape[1]
    share = out_ref.shape[2]
    for side in range(2):
        cols = slice(side * share, (side + 1) * share)
        total = turned(h0[0:part, :], near_ref[0, :, cols])
        for step, ref in enumerate((h0, h1, h2, h3)):
            if step:
                total += turned(ref[0:part, :], near_ref[step, :, cols])
            total += turned(ref[part : 2 * part, :], far_ref[step, :, cols])
        out_ref[side] = total.astype(BF16)


def combine_kernel(sc, ret_ref, high_ref, low_ref, tok_ref, gain_ref, proj_ref, out_ref):
    mixed = jnp.dot(high_ref[...], ret_ref[...], preferred_element_type=F32)
    mixed += jnp.dot(low_ref[...], ret_ref[...], preferred_element_type=F32)
    feat = (tok_ref[...].astype(F32) + mixed).astype(BF16).astype(F32)
    square = jnp.sum(feat * feat, axis=1, keepdims=True)
    part = jnp.dot(
        (feat * gain_ref[...]).astype(BF16), proj_ref[...], preferred_element_type=F32
    )
    tiles, block, _ = out_ref.shape
    count, channels = part.shape
    lane = iota((count, 128), 1)
    high = square.astype(BF16).astype(F32)
    extra = jnp.where(lane == 0, high, jnp.where(lane == 1, square - high, 0.0))
    own = count // tiles
    border = (block - own) // 2
    for tile in range(tiles):
        begin = tile * own - border
        low, top = max(begin, 0), min(begin + block, count)
        for value, cols in (
            (part, slice(0, channels)),
            (extra, slice(channels, channels + 128)),
        ):
            pieces = [value[low:top, :]]
            if low > begin:
                pieces = [jnp.zeros((low - begin, value.shape[1]), F32)] + pieces
            if top < begin + block:
                pieces = pieces + [jnp.zeros((begin + block - top, value.shape[1]), F32)]
            joined = pieces[0] if len(pieces) == 1 else jnp.concatenate(pieces, axis=0)
            out_ref[tile, :, cols] = joined.astype(BF16)


def convolved(field, weights, rows):
    sums = []
    for col_step in range(3):
        total = None
        for row_step in range(3):
            term = jnp.dot(
                field[row_step * 16 : row_step * 16 + rows, :],
                weights(row_step, col_step),
                preferred_element_type=F32,
            )
            total = term if total is None else total + term
        sums.append(total)
    col = iota(sums[0].shape, 0) & 15
    left = jnp.where(col == 0, 0.0, pltpu.roll(sums[0], 1, 0))
    right = jnp.where(col == 15, 0.0, pltpu.roll(sums[2], rows - 1, 0))
    return sums[1] + left + right


def cache_kernel(sc, cache_ref, above_ref, below_ref, weight_ref, bias_ref, out_ref):
    head = sc[2]
    older = lax.rem(head + 2, 3)
    total = jnp.broadcast_to(bias_ref[...], out_ref.shape)
    for step, slot in ((0, older), (1, head)):
        field = jnp.concatenate([above_ref[slot], cache_ref[slot], below_ref[slot]], axis=0)
        total = total + convolved(field, lambda r, c: weight_ref[step, r, c], out_ref.shape[0])
    out_ref[...] = total


def tail_kernel(sc, arr_ref, past_ref, time_ref, space_ref, bias_ref, out_ref):
    tile = sc[0]
    total = arr_ref[0].astype(F32)
    for source in range(1, arr_ref.shape[0]):
        total = total + arr_ref[source].astype(F32)
    channels = out_ref.shape[1]
    square = total[:, channels : channels + 1] + total[:, channels + 1 : channels + 2]
    scale = lax.rsqrt(square / 4096.0 + EPS)
    coarse = (total[:, :channels] * scale).astype(BF16)
    block = coarse.shape[0]
    pixel = iota((4 * block, block), 0)
    spread = jnp.where(
        iota((4 * block, block), 1) == (pixel >> 5) * 8 + ((pixel & 15) >> 1), 1.0, 0.0
    ).astype(BF16)
    fine = jnp.dot(spread, coarse, preferred_element_type=F32)
    field = fine.astype(BF16)
    rows = past_ref.shape[0]
    first = past_ref[...] + convolved(field, lambda r, c: time_ref[0, r, c], rows)
    active = first / (1.0 + jnp.exp(-first))
    place = (iota(active.shape, 0) >> 4) + tile * 8 - 1
    active = jnp.where((place >= 0) & (place < 64), active, 0.0).astype(BF16)
    own = out_ref.shape[0]
    second = convolved(active, lambda r, c: space_ref[r, c], own)
    out_ref[...] = (fine[32 : 32 + own, :] + second + bias_ref[...]).astype(BF16)


def in_hbm(x):
    return pltpu.with_memory_space_constraint(x, pltpu.HBM)


def flipped(x, bits):
    return lax.ppermute(x, EXP, [(i, i ^ bits) for i in range(8)])


def swapped(x, axis):
    return lax.ppermute(x, axis, [(0, 1), (1, 0)])


def body(
    tokens,
    routes,
    gates,
    w_gate,
    w_up,
    w_down,
    feat_gain,
    w_proj,
    conv_time,
    bias_time,
    conv_space,
    bias_space,
    frame_cache,
    cache_head,
):
    tile = lax.axis_index(EXP).astype(jnp.int32)
    half = tile >> 2
    quarter = (tile & 3) ^ (half << 1)
    scalars = jnp.stack([tile, half, cache_head[0], quarter, quarter ^ 1, quarter ^ 2, quarter ^ 3])
    count, width = tokens.shape[1:]
    hid = w_gate.shape[2]
    channels = w_proj.shape[1]
    fourth = width // 4
    share = width // 8
    own_gate, own_up = w_gate[0].T, w_up[0].T

    with jax.named_scope("exchange_weights"):
        pairs = [(i, i ^ 6) for i in range(8)]
        other_gate = lax.ppermute(own_gate, EXP, pairs)
        slabs = call(
            slab_kernel,
            "slabs",
            scalars,
            (w_down[0],) * 4,
            [pl.BlockSpec((hid, fourth), lambda i, s, k=k: (0, s[3 + k])) for k in range(4)],
            [jax.ShapeDtypeStruct((hid, fourth), BF16)] * 4,
        )
        near_1, near_2, near_3 = [flipped(slabs[k], k) for k in (1, 2, 3)]
        columns = call(
            columns_kernel,
            "columns",
            scalars,
            (in_hbm(routes[0].T), in_hbm(gates[0].T)),
            [whole((2, count))] * 2,
            jax.ShapeDtypeStruct((count, 128), F32),
        )
        later, other_gate, columns = lax.optimization_barrier((own_up, other_gate, columns))
        other_up = lax.ppermute(later, EXP, pairs)

    with jax.named_scope("cache"):
        frames = frame_cache.reshape(3, 128, channels)
        above = lax.ppermute(frames[:, 96:], EXP, [(i, i + 1) for i in range(7)])
        below = lax.ppermute(frames[:, :32], EXP, [(i + 1, i) for i in range(7)])
        frames, *_ = lax.optimization_barrier((frames, near_1, near_2, near_3))
        past = call(
            cache_kernel,
            "cache",
            scalars,
            (
                in_hbm(frames),
                above,
                below,
                in_hbm(conv_time),
                in_hbm(bias_time.reshape(1, channels)),
            ),
            [
                whole(frames.shape),
                whole(above.shape),
                whole(below.shape),
                pl.BlockSpec((2, 3, 3, channels, channels), lambda i, s: (0, 0, 0, 0, 0)),
                whole((1, channels)),
            ],
            jax.ShapeDtypeStruct((160, channels), F32),
            cost=pl.CostEstimate(flops=16000 * 10**6, bytes_accessed=80 * 10**6, transcendentals=0),
        )

    with jax.named_scope("dispatch"):
        outgoing = call(
            dispatch_kernel,
            "dispatch",
            scalars,
            (in_hbm(routes[0].T), in_hbm(tokens[0])),
            [whole((2, count)), pl.BlockSpec((count, fourth), lambda i, s: (0, s[3]))],
            jax.ShapeDtypeStruct((512, fourth), BF16),
        )
        arrived = lax.all_to_all(
            outgoing.reshape(32, 16, fourth), "sess", 0, 0, tiled=True
        ).reshape(512, fourth)
        columns, _ = lax.optimization_barrier((columns, other_gate))
        high, low = call(
            weights_kernel,
            "weights",
            scalars,
            (columns,),
            [whole((count, 128))],
            [jax.ShapeDtypeStruct((count, 1024), BF16)] * 2,
            cost=pl.CostEstimate(flops=12000 * 10**6, bytes_accessed=60 * 10**6, transcendentals=0),
        )

    with jax.named_scope("gather"):
        arrived, near_1, near_2, near_3, high, low = lax.optimization_barrier(
            (arrived, near_1, near_2, near_3, high, low)
        )
        near = jnp.stack([slabs[0], near_2, near_1, near_3])
        from_y = swapped(arrived, "yl")
        from_x = swapped(arrived, "x")
        from_x, from_y, past = lax.optimization_barrier((from_x, from_y, past))
        corner_top = swapped(from_y[:256], "x")
        corner_low = swapped(from_x[256:], "yl")
        arrived, from_x, from_y = lax.optimization_barrier((arrived, from_x, from_y))
        near, other_up = lax.optimization_barrier((near, other_up))
        far = flipped(near, 6)

    with jax.named_scope("experts"):
        weights = (own_gate, other_gate, own_up, other_up)
        pair = [jax.ShapeDtypeStruct((2 * hid, 512), F32)] * 2
        scratch = [pltpu.VMEM((2 * hid, fourth), BF16)] * 2
        acc = whole((2 * hid, 512))
        gate, up = call(
            first_kernel,
            "first",
            scalars,
            (arrived, from_x, from_y, *weights),
            [whole((512, fourth))] * 3 + [whole((hid, width))] * 4,
            pair,
            scratch,
            24,
        )
        hidden = call(
            last_kernel,
            "hidden",
            scalars,
            (corner_top, corner_low, *weights, gate, up),
            [whole((256, fourth))] * 2
            + [pl.BlockSpec((hid, fourth), lambda i, s: (0, s[6]))] * 4
            + [acc, acc],
            jax.ShapeDtypeStruct((2 * hid, 512), BF16),
            scratch,
            16,
        )

    with jax.named_scope("hidden_gather"):
        hidden_y = swapped(hidden, "yl")
        hidden_x = swapped(hidden, "x")
        hidden_c = lax.ppermute(hidden, ("yl", "x"), [(i, 3 - i) for i in range(4)])

    with jax.named_scope("down"):
        answer = call(
            down_kernel,
            "down",
            scalars,
            (hidden, hidden_y, hidden_x, hidden_c, near, far),
            [whole((2 * hid, 512))] * 4 + [whole((4, hid, fourth))] * 2,
            jax.ShapeDtypeStruct((2, 512, share), BF16),
            [],
            20,
        )
        returned = lax.all_to_all(
            answer.reshape(64, 16, share),
            ("sess",) + EXP,
            0,
            0,
            axis_index_groups=[
                [s * 8 + 4 * h + (c ^ (2 * h)) for h in range(2) for s in range(32)]
                for c in range(4)
            ],
            tiled=True,
        ).reshape(1024, share)

    with jax.named_scope("combine"):
        blocks = call(
            combine_kernel,
            "combine",
            scalars,
            (returned, high, low, tokens[0], feat_gain.reshape(1, width), w_proj),
            [
                whole((1024, share)),
                whole((count, 1024)),
                whole((count, 1024)),
                pl.BlockSpec((count, share), lambda i, s: (0, s[3] * 2 + s[1])),
                pl.BlockSpec((1, share), lambda i, s: (0, s[3] * 2 + s[1])),
                pl.BlockSpec((share, channels), lambda i, s: (s[3] * 2 + s[1], 0)),
            ],
            jax.ShapeDtypeStruct((8, 48, channels + 128), BF16),
        )
        blocks = lax.all_to_all(blocks, EXP, 0, 0, tiled=True)

    with jax.named_scope("decode"):
        out = call(
            tail_kernel,
            "decode",
            scalars,
            (blocks, past, conv_time, conv_space, bias_space.reshape(1, channels)),
            [
                whole(blocks.shape),
                whole((160, channels)),
                pl.BlockSpec((1, 3, 3, channels, channels), lambda i, s: (2, 0, 0, 0, 0)),
                whole(conv_space.shape),
                whole((1, channels)),
            ],
            jax.ShapeDtypeStruct((128, channels), BF16),
        )
    return out.reshape(1, 8, 16, channels)


def solution(mesh):
    finer = Mesh(
        mesh.devices.reshape(mesh.shape["sess"], 2, 2, 2), ("sess", "yh", "yl", "x")
    )
    return jax.shard_map(
        body,
        mesh=finer,
        in_specs=(
            P("sess", None, None),
            P("sess", None, None),
            P("sess", None, None),
            P("sess", None, EXP),
            P("sess", None, EXP),
            P("sess", EXP, None),
            P(),
            P(),
            P(),
            P(),
            P(),
            P(),
            P(None, "sess", EXP, None, None),
            P("sess"),
        ),
        out_specs=P("sess", EXP, None, None),
        check_vma=False,
    )
```
